32 devices in a mesh: dom: 16 (over z, y, core), orb: 2 (over x).
Axes of the slice: x: 2, y: 2, z: 4, core: 2. Of those that a mesh axis runs over, the one named last changes fastest.
Arguments:
- orbitals: float32 [6144, 1024], P('dom', 'orb'), may hold values from -6 to 6
- cell_mats: float32 [16, 512, 512], P('dom'), as said below
- cell_map: int32 [16, 512], P('dom'), may hold values from 0 to 511, as said below
Outputs:
- rotated: float32 [6144, 1024], P(('dom', 'orb'))
The draws below stay inside these ranges and needn't reach their ends.
Inputs may be any that keep to these rules, and one draw needn't show every extreme that they name: `cell_map`: cell c belongs to domain c. Its 512 entries are distinct. Entries below 384 name the domain's own nodes, each used by some cell of the domain; an entry j >= 384 names own node j - 384 of the next domain, and every such j is used by some cell of the domain. `cell_mats`: each cell matrix is symmetric.
All inputs are finite; a program needn't handle non-finite values.
Results may differ from the reference program's by a relative error of at most 0.00013.
Values sent between devices are 32-bit elements; how exact they have to be, the bound alone decides.
No kernel may reach another device: no remote copies, remote signals or barrier semaphores. Data moves between devices by JAX's collectives and lax.ppermute only.
A program may use at most 64 MiB of HBM per device.

```python
import jax
import jax.numpy as jnp
from jax import lax

NPC = 512
ORBS = 1024
DEGREE = 5
CELL_DEV = 1
HALO = 128
OWN_CELL = 384
OWN = 384
CELLS = 16
NODES = 6144
N_DOM = 16


def draw_cell_mats(key, part):
    first_key, second_key = jax.random.split(key)
    base = jnp.clip(jax.random.normal(first_key, (CELLS, NPC, NPC), jnp.float32), -4.0, 4.0)
    diagonal = jax.random.uniform(second_key, (CELLS, NPC), jnp.float32, 0.5, 2.0)
    symmetric = (base + jnp.swapaxes(base, 1, 2)) * (0.5 / NPC ** 0.5)
    eye_mask = jnp.eye(NPC, dtype=jnp.float32)
    return symmetric + eye_mask[None, :, :] * diagonal[:, :, None]


def draw_cell_map(key, part):

    def one_cell(cell_idx):
        cell_key = jax.random.fold_in(key, cell_idx)
        local_idx = cell_idx % CELL_DEV
        owned = local_idx * OWN_CELL + jnp.arange(OWN_CELL, dtype=jnp.int32)
        picked = jax.random.permutation(jax.random.fold_in(cell_key, 1), OWN_CELL)[:HALO].astype(jnp.int32)
        from_next = picked + (local_idx + 1) * OWN_CELL
        borrowed = OWN + jnp.arange(HALO, dtype=jnp.int32)
        shared = jnp.where(local_idx == CELL_DEV - 1, borrowed, from_next)
        joined = jnp.concatenate([owned, shared.astype(jnp.int32)])
        order = jax.random.permutation(jax.random.fold_in(cell_key, 2), NPC)
        return joined[order].astype(jnp.int32)
    return jax.vmap(one_cell)(jnp.arange(CELLS, dtype=jnp.int32))


def block_scale(key, dims, cuts, low, high):
    level, own = 1.0, jax.random.fold_in(key, 6)
    for axis_at, parts in cuts:
        draws = jnp.exp(jax.random.uniform(jax.random.fold_in(own, axis_at), (parts,), jnp.float32, low / len(cuts), high / len(cuts)))
        level = level * jnp.repeat(draws, dims[axis_at] // parts).reshape([-1 if axis == axis_at else 1 for axis in range(len(dims))])
    return level


def centred(own_key, shape, width, limit, pieces=(), kind=jnp.bfloat16):
    array = jax.random.normal(own_key, shape, jnp.float32) * width
    if len(pieces) > 0:
        array = block_scale(own_key, shape, pieces, -0.22, 0.18) * array
    return jnp.clip(array, min=-limit, max=limit).astype(kind)


def setup_inputs(seed: int = 0) -> dict:
    key_list = jax.random.split(jax.random.key(seed), 4)
    return {
        "orbitals": centred(key_list[0], (NODES, ORBS), 1.0, 6.0, ((0, 16), (1, 2)), jnp.float32),
        "cell_mats": draw_cell_mats(jax.random.fold_in(key_list[3], 71), 0),
        "cell_map": draw_cell_map(jax.random.fold_in(key_list[3], 71), 0),
    }


filter_center = 2.0
filter_half = 3.5

def global_map(cell_map):
    owner = (jnp.arange(CELLS, dtype=jnp.int32) // CELL_DEV)[:, None]
    following = (owner + 1) % N_DOM
    mapped = jnp.where(cell_map < OWN, owner * OWN + cell_map, following * OWN + cell_map - OWN)
    return mapped.astype(jnp.int32)

def apply_operator(vectors, cell_mats, nodes_of):

    def visit(summed, inputs):
        matrix, node_idx = inputs
        gathered = jnp.take(vectors, node_idx, axis=0)
        product = jnp.dot(matrix.astype(jnp.float32), gathered.astype(jnp.float32), precision=lax.Precision.HIGHEST, preferred_element_type=jnp.float32)
        return (summed.at[node_idx].add(product), None)
    summed, ignored = lax.scan(visit, jnp.zeros(vectors.shape, jnp.float32), (cell_mats, nodes_of))
    return summed

def reference(orbitals, cell_mats, cell_map):
    nodes_of = global_map(cell_map)
    previous = orbitals
    current = (apply_operator(orbitals, cell_mats, nodes_of) - filter_center * orbitals) / filter_half
    for order in range(1, DEGREE):
        advanced = 2.0 * (apply_operator(current, cell_mats, nodes_of) - filter_center * current) / filter_half - previous
        previous, current = (current, advanced)
    gram = jnp.einsum('nk,nj->kj', current, current, precision=lax.Precision.HIGHEST) / NODES
    lower = jnp.linalg.cholesky(gram)
    solved = lax.linalg.triangular_solve(lower, current.T, left_side=True, lower=True)
    return solved.T
```

```python
import jax
import jax.numpy as jnp
from jax import lax
from jax.experimental import pallas as pl
from jax.experimental.pallas import tpu as pltpu
from jax.sharding import PartitionSpec as P

DEGREE = 5

filter_center = 2.0
filter_half = 3.5

F32, BF16 = jnp.float32, jnp.bfloat16
LANES, SUB = 128, 8
VMEM_BYTES = 48 << 20


def kernel_call(body, out_shape, scratch=()):
    return pl.pallas_call(
        body,
        out_shape=out_shape,
        scratch_shapes=list(scratch),
        compiler_params=pltpu.CompilerParams(vmem_limit_bytes=VMEM_BYTES),
    )


def f32(*shape):
    return jax.ShapeDtypeStruct(shape, F32)


def bf16(*shape):
    return jax.ShapeDtypeStruct(shape, BF16)


def split(v):
    hi = v.astype(BF16)
    return hi, (v - hi.astype(F32)).astype(BF16)


def contract(a, b, dims):
    return lax.dot_general(a, b, (dims, ((), ())), preferred_element_type=F32)


def product(a, b, dims):
    (a_hi, a_lo), (b_hi, b_lo) = a, b
    return contract(a_hi, b_hi, dims) + (contract(a_hi, b_lo, dims) + contract(a_lo, b_hi, dims))


NN = ((1,), (0,))
NT = ((1,), (1,))


def order_kernel(map_ref, cell_ref, hi_ref, lo_ref):
    size = cell_ref.shape[1]
    node = lax.broadcasted_iota(jnp.int32, (size, size), 0)
    pick = jnp.where(node == map_ref[...], 1.0, 0.0).astype(BF16)
    for half, out_ref in zip(split(cell_ref[0]), (hi_ref, lo_ref)):
        rows = contract(pick, half, NN).astype(BF16)
        out_ref[...] = contract(rows, pick, NT).astype(BF16)


def step_kernel(order, own, hi_ref, lo_ref, *refs):
    size = hi_ref.shape[0]
    halo = size - own
    if order == 0:
        own_ref, bottom_ref = refs[:2]
        vec = jnp.concatenate([own_ref[...], bottom_ref[...]], axis=0)
        outs = refs[2:]
    else:
        part_ref, top_ref, bottom_ref = refs[:3]
        vec = jnp.concatenate(
            [
                part_ref[:halo, :] + top_ref[...],
                part_ref[halo:own, :],
                part_ref[own:, :] + bottom_ref[...],
            ],
            axis=0,
        )
        outs = refs[3:]
    if order > 0:
        before_ref, outs = outs[0], outs[1:]
    scale = (1.0 if order == 0 else 2.0) / filter_half
    applied = product((hi_ref[...], lo_ref[...]), split(vec), NN) * scale
    part = applied - (filter_center * scale) * vec
    if order > 0:
        part = part - before_ref[...]
    if order == DEGREE - 1:
        next_ref, down_ref = outs
        next_ref[...] = part[:own]
    else:
        now_ref, next_ref, up_ref, down_ref = outs
        now_ref[...] = vec
        next_ref[...] = part
        up_ref[...] = applied[:halo]
    down_ref[...] = applied[own:]


def shifted(block, axis, distance):
    count = lax.axis_size(axis)
    route = [((i - distance) % count, i) for i in range(count)]
    return lax.ppermute(block, axis, route)


def filtered_columns(orbitals, matrix):
    own, cols = orbitals.shape
    size = matrix[0].shape[0]
    halo = size - own
    bottom = shifted(orbitals[:halo], "dom", -1)
    state = (orbitals, bottom)
    for order in range(DEGREE):
        last = order == DEGREE - 1
        outs = [f32(own if last else size, cols)]
        if not last:
            outs = [f32(size, cols)] + outs + [f32(halo, cols)]
        outs.append(f32(halo, cols))
        body = lambda *refs, order=order: step_kernel(order, own, *refs)
        got = kernel_call(body, outs)(*matrix, *state)
        if last:
            part, down = got
            top = shifted(down, "dom", 1)
            return jnp.concatenate([part[:halo] + top, part[halo:]], axis=0)
        now, part, up, down = got
        top = shifted(down, "dom", 1)
        bottom = shifted(up, "dom", -1)
        state = (part, top, bottom, now)


def gram_kernel(rows_ref, out_ref):
    hi, lo = split(rows_ref[...].T)
    panels = hi.shape[0] // LANES
    at = 0
    for p in range(panels):
        cut = slice(p * LANES, (p + 1) * LANES)
        below = hi.shape[0] - p * LANES
        out_ref[at : at + below, :] = product((hi[p * LANES :], lo[p * LANES :]), (hi[cut], lo[cut]), NT)
        at += below


def exchanged(block, axis, bit):
    route = [(i, i ^ bit) for i in range(lax.axis_size(axis))]
    return lax.ppermute(block, axis, route)


def summed(block, stages):
    for axis, bit in stages:
        half = block.shape[0] // 2
        upper = (lax.axis_index(axis) & bit) != 0
        pair = block.reshape(2, half, block.shape[1])
        keep = jnp.where(upper, pair[1], pair[0])
        send = jnp.where(upper, pair[0], pair[1])
        block = keep + exchanged(send, axis, bit)
    for axis, bit in reversed(stages):
        upper = (lax.axis_index(axis) & bit) != 0
        other = exchanged(block, axis, bit)
        block = jnp.concatenate([jnp.where(upper, other, block), jnp.where(upper, block, other)], axis=0)
    return block


def bits(axis):
    count = lax.axis_size(axis)
    return [(axis, 1 << i) for i in range(count.bit_length() - 1)]


def inverse_factor(block, out_ref):
    size = block.shape[0]
    rows = [block[t : t + SUB] for t in range(0, size, SUB)]
    sub = lax.broadcasted_iota(jnp.int32, (SUB, size), 0)
    lane = lax.broadcasted_iota(jnp.int32, (SUB, size), 1)
    for b in range(size // SUB):
        at = b * SUB
        here = (lane >= at) & (lane < at + SUB)
        top = rows[b]
        cols = [jnp.broadcast_to(top[:, at + k : at + k + 1], (SUB, size)) for k in range(SUB)]
        top = jnp.where(here, jnp.where(lane - at == sub, 1.0, 0.0), top)
        scale = jnp.zeros((SUB, size), F32)
        done = jnp.zeros((SUB, size), F32)
        for k in range(SUB):
            pivot = jnp.broadcast_to(cols[k][k : k + 1], (SUB, size))
            inverse = 1.0 / pivot
            row = jnp.broadcast_to(top[k : k + 1], (SUB, size))
            done = jnp.where(sub == k, row * lax.rsqrt(pivot), done)
            scale = jnp.where(sub == k, inverse, scale)
            ratio = jnp.where(sub == k, 0.0, cols[k] * inverse)
            top = top - ratio * row
            for m in range(k + 1, SUB):
                cols[m] = cols[m] - ratio * jnp.broadcast_to(cols[m][k : k + 1], (SUB, size))
        out_ref[at : at + SUB, :] = jnp.where(lane < at + SUB, done, 0.0)
        top = top * scale
        for t in range(b + 1, size // SUB):
            left = rows[t]
            kept = jnp.where(here, 0.0, left)
            for k in range(SUB):
                column = jnp.broadcast_to(left[:, at + k : at + k + 1], (SUB, size))
                kept = kept - column * jnp.broadcast_to(top[k : k + 1], (SUB, size))
            rows[t] = kept


def factor_kernel(scale, gram_ref, rows_ref, out_ref, work_ref, hi_ref, lo_ref, inverse_ref):
    panels, total = work_ref.shape[:2]
    size = panels * LANES
    at = 0
    for p in range(panels):
        below = size - p * LANES
        work_ref[p, size - below : size, :] = gram_ref[at : at + below, :] * scale
        work_ref[p, size:, :] = rows_ref[:, p * LANES : (p + 1) * LANES]
        if p > 0:
            work_ref[p, : size - below, :] = jnp.zeros((size - below, LANES), F32)
        at += below

    def panel(p, carry):
        offset = pl.multiple_of(p * LANES, LANES)

        def update(k, inner):
            mine = pl.ds(offset, LANES)
            pair = (hi_ref[k, mine, :], lo_ref[k, mine, :])
            work_ref[p] = work_ref[p] - product((hi_ref[k], lo_ref[k]), pair, NT)
            return inner

        lax.fori_loop(0, p, update, 0)
        inverse_factor(work_ref[p, pl.ds(offset, LANES), :], inverse_ref)
        solved = product(split(work_ref[p]), split(inverse_ref[...]), NT)
        hi_ref[p], lo_ref[p] = split(solved)
        work_ref[p] = solved
        return carry

    lax.fori_loop(0, panels, panel, 0)
    for p in range(panels):
        out_ref[:, p * LANES : (p + 1) * LANES] = work_ref[p, size:, :]


def body(orbitals, cell_mats, cell_map):
    own, cols = orbitals.shape
    size = cell_mats.shape[1]
    node_total = own * lax.axis_size("dom")
    matrix = kernel_call(order_kernel, [bf16(size, size)] * 2)(cell_map, cell_mats)
    current = filtered_columns(orbitals, matrix)
    regrouped = lax.all_to_all(current, "orb", split_axis=0, concat_axis=1, tiled=True)
    count, width = regrouped.shape
    panels = width // LANES
    packed = LANES * panels * (panels + 1) // 2
    gram = kernel_call(gram_kernel, f32(packed, LANES))(regrouped)
    dom = bits("dom")
    gram = summed(gram, dom[:1] + bits("orb") + dom[1:])
    scratch = [
        pltpu.VMEM((panels, width + count, LANES), F32),
        pltpu.VMEM((panels, width + count, LANES), BF16),
        pltpu.VMEM((panels, width + count, LANES), BF16),
        pltpu.VMEM((LANES, LANES), F32),
    ]
    factor = lambda *refs: factor_kernel(1.0 / node_total, *refs)
    return kernel_call(factor, f32(count, width), scratch)(gram, regrouped)


def solution(mesh):
    placed = (P("dom", "orb"), P("dom", None, None), P("dom", None))
    return jax.shard_map(
        body, mesh=mesh, in_specs=placed, out_specs=P(("dom", "orb"), None), check_vma=False
    )
```

```python
import jax
import jax.numpy as jnp
from jax import lax
from jax.experimental import pallas as pl
from jax.experimental.pallas import tpu as pltpu
from jax.sharding import PartitionSpec as P

DEGREE = 5

filter_center = 2.0
filter_half = 3.5

F32, BF16 = jnp.float32, jnp.bfloat16
LANES, SUB = 128, 8
VMEM_BYTES = 48 << 20


def kernel_call(body, out_shape, scratch=()):
    return pl.pallas_call(
        body,
        out_shape=out_shape,
        scratch_shapes=list(scratch),
        compiler_params=pltpu.CompilerParams(vmem_limit_bytes=VMEM_BYTES),
    )


def f32(*shape):
    return jax.ShapeDtypeStruct(shape, F32)


def bf16(*shape):
    return jax.ShapeDtypeStruct(shape, BF16)


def split(v):
    hi = v.astype(BF16)
    return hi, (v - hi.astype(F32)).astype(BF16)


def contract(a, b, dims):
    return lax.dot_general(a, b, (dims, ((), ())), preferred_element_type=F32)


def product(a, b, dims):
    (a_hi, a_lo), (b_hi, b_lo) = a, b
    return contract(a_hi, b_hi, dims) + (contract(a_hi, b_lo, dims) + contract(a_lo, b_hi, dims))


NN = ((1,), (0,))
NT = ((1,), (1,))


def order_kernel(map_ref, cell_ref, hi_ref, lo_ref):
    size = cell_ref.shape[1]
    node = lax.broadcasted_iota(jnp.int32, (size, size), 0)
    pick = jnp.where(node == map_ref[...], 1.0, 0.0).astype(BF16)
    for half, out_ref in zip(split(cell_ref[0]), (hi_ref, lo_ref)):
        rows = contract(pick, half, NN).astype(BF16)
        out_ref[...] = contract(rows, pick, NT).astype(BF16)


def step_kernel(order, own, hi_ref, lo_ref, *refs):
    size = hi_ref.shape[0]
    halo = size - own
    if order == 0:
        own_ref, bottom_ref = refs[:2]
        vec = jnp.concatenate([own_ref[...], bottom_ref[...]], axis=0)
        outs = refs[2:]
    else:
        part_ref, top_ref, bottom_ref = refs[:3]
        vec = jnp.concatenate(
            [
                part_ref[:halo, :] + top_ref[...],
                part_ref[halo:own, :],
                part_ref[own:, :] + bottom_ref[...],
            ],
            axis=0,
        )
        outs = refs[3:]
    if order > 0:
        before_ref, outs = outs[0], outs[1:]
    scale = (1.0 if order == 0 else 2.0) / filter_half
    applied = product((hi_ref[...], lo_ref[...]), split(vec), NN) * scale
    part = applied - (filter_center * scale) * vec
    if order > 0:
        part = part - before_ref[...]
    if order == DEGREE - 1:
        next_ref, down_ref = outs
        next_ref[...] = part[:own]
    else:
        now_ref, next_ref, up_ref, down_ref = outs
        now_ref[...] = vec
        next_ref[...] = part
        up_ref[...] = applied[:halo]
    down_ref[...] = applied[own:]


def shifted(block, axis, distance):
    count = lax.axis_size(axis)
    route = [((i - distance) % count, i) for i in range(count)]
    return lax.ppermute(block, axis, route)


def filtered_columns(orbitals, matrix):
    own, cols = orbitals.shape
    size = matrix[0].shape[0]
    halo = size - own
    bottom = shifted(orbitals[:halo], "dom", -1)
    state = (orbitals, bottom)
    for order in range(DEGREE):
        last = order == DEGREE - 1
        outs = [f32(own if last else size, cols)]
        if not last:
            outs = [f32(size, cols)] + outs + [f32(halo, cols)]
        outs.append(f32(halo, cols))
        body = lambda *refs, order=order: step_kernel(order, own, *refs)
        got = kernel_call(body, outs)(*matrix, *state)
        if last:
            part, down = got
            top = shifted(down, "dom", 1)
            return part, top
        now, part, up, down = got
        top = shifted(down, "dom", 1)
        bottom = shifted(up, "dom", -1)
        state = (part, top, bottom, now)


def gram_kernel(rows_ref, out_ref):
    hi, lo = split(rows_ref[...].T)
    panels = hi.shape[0] // LANES
    at = 0
    for p in range(panels):
        cut = slice(p * LANES, (p + 1) * LANES)
        below = hi.shape[0] - p * LANES
        out_ref[at : at + below, :] = product((hi[p * LANES :], lo[p * LANES :]), (hi[cut], lo[cut]), NT)
        at += below


def half_gram(mine, other, second, out_ref, base_ref):
    own, own_lo = split(mine.T)
    other, other_lo = split(other.T)
    cols = own.shape[0]
    half = cols // 2

    def put(at, value):
        span = slice(at, at + value.shape[0])
        out_ref[span, :] = value if base_ref is None else base_ref[span, :] + value

    at = 0
    for p in range(0, cols, LANES):
        put(at, product((own[p:], own_lo[p:]), (own[p : p + LANES], own_lo[p : p + LANES]), NT))
        at += cols - p

    def cross(left, right):
        for i, p in enumerate(range(0, cols, LANES)):
            cut = slice(p, p + LANES)
            put(at + i * half, product(left, (right[0][cut], right[1][cut]), NT))

    @pl.when(second == 0)
    def _():
        cross((other[:half], other_lo[:half]), (own, own_lo))

    @pl.when(second == 1)
    def _():
        cross((own[half:], own_lo[half:]), (other, other_lo))


def low_gram_kernel(halo, second_ref, mine_ref, other_ref, out_ref):
    half_gram(mine_ref[halo:, :], other_ref[...], second_ref[0], out_ref, None)


def high_gram_kernel(second_ref, part_ref, top_ref, other_ref, base_ref, out_ref):
    halo = top_ref.shape[0]
    half_gram(part_ref[:halo, :] + top_ref[...], other_ref[...], second_ref[0], out_ref, base_ref)


def exchanged(block, axis, mask):
    route = [(i, i ^ mask) for i in range(lax.axis_size(axis))]
    return lax.ppermute(block, axis, route)


def bits(axis):
    count = lax.axis_size(axis)
    return [(axis, 1 << i, 2) for i in range(count.bit_length() - 1)]


def rank(axis, unit, count):
    return (lax.axis_index(axis) // unit) % count


def scattered(block, stages):
    for axis, unit, count in stages:
        mine = rank(axis, unit, count)
        pieces = block.reshape(count, -1, block.shape[-1])
        total = lax.dynamic_index_in_dim(pieces, mine, keepdims=False)
        for d in range(1, count):
            piece = lax.dynamic_index_in_dim(pieces, mine ^ d, keepdims=False)
            total = total + exchanged(piece, axis, d * unit)
        block = total
    return block


def gathered(block, stage):
    axis, unit, count = stage
    mine = rank(axis, unit, count)
    pieces = jnp.stack([block] + [exchanged(block, axis, d * unit) for d in range(1, count)])
    bit = 1
    while bit < count:
        pair = pieces.reshape((count // (2 * bit), 2, bit) + block.shape)
        pieces = jnp.where((mine & bit) != 0, pair[:, ::-1], pair).reshape(pieces.shape)
        bit *= 2
    return pieces


def summed(block, stages):
    width = block.shape[-1]
    block = scattered(block, stages)
    for stage in reversed(stages):
        block = gathered(block, stage).reshape(-1, width)
    return block


def inverse_factor(block, out_ref):
    size = block.shape[0]
    rows = [block[t : t + SUB] for t in range(0, size, SUB)]
    sub = lax.broadcasted_iota(jnp.int32, (SUB, size), 0)
    lane = lax.broadcasted_iota(jnp.int32, (SUB, size), 1)
    for b in range(size // SUB):
        at = b * SUB
        here = (lane >= at) & (lane < at + SUB)
        top = rows[b]
        cols = [jnp.broadcast_to(top[:, at + k : at + k + 1], (SUB, size)) for k in range(SUB)]
        top = jnp.where(here, jnp.where(lane - at == sub, 1.0, 0.0), top)
        scale = jnp.zeros((SUB, size), F32)
        done = jnp.zeros((SUB, size), F32)
        for k in range(SUB):
            pivot = jnp.broadcast_to(cols[k][k : k + 1], (SUB, size))
            inverse = 1.0 / pivot
            row = jnp.broadcast_to(top[k : k + 1], (SUB, size))
            done = jnp.where(sub == k, row * lax.rsqrt(pivot), done)
            scale = jnp.where(sub == k, inverse, scale)
            ratio = jnp.where(sub == k, 0.0, cols[k] * inverse)
            top = top - ratio * row
            for m in range(k + 1, SUB):
                cols[m] = cols[m] - ratio * jnp.broadcast_to(cols[m][k : k + 1], (SUB, size))
        out_ref[at : at + SUB, :] = jnp.where(lane < at + SUB, done, 0.0)
        top = top * scale
        for t in range(b + 1, size // SUB):
            left = rows[t]
            kept = jnp.where(here, 0.0, left)
            for k in range(SUB):
                column = jnp.broadcast_to(left[:, at + k : at + k + 1], (SUB, size))
                kept = kept - column * jnp.broadcast_to(top[k : k + 1], (SUB, size))
            rows[t] = kept


def packed_block(gram_ref, row, col, panels):
    at = sum(panels - p for p in range(col)) + row - col
    return gram_ref[at * LANES : (at + 1) * LANES, :]


def halved_block(gram_ref, row, col, panels):
    mid = panels // 2
    triangle = mid * (mid + 1) // 2
    if (row < mid) == (col < mid):
        second, row, col = int(row >= mid), row % mid, col % mid
        at = sum(mid - p for p in range(col)) + row - col
    else:
        second, at = divmod(row - mid, mid // 2)
        at += triangle + col * (mid // 2)
    chunk = gram_ref.shape[2] // LANES
    part, at = divmod(at, chunk)
    return gram_ref[part, second, at * LANES : (at + 1) * LANES, :]


def factor_kernel(scale, block_of, gram_ref, rows_ref, out_ref, work_ref, hi_ref, lo_ref, inverse_ref):
    panels, total = work_ref.shape[:2]
    size = panels * LANES
    for p in range(panels):
        for r in range(panels):
            block = block_of(gram_ref, r, p, panels) * scale if r >= p else jnp.zeros((LANES, LANES), F32)
            work_ref[p, r * LANES : (r + 1) * LANES, :] = block
        work_ref[p, size:, :] = rows_ref[:, p * LANES : (p + 1) * LANES]

    def panel(p, carry):
        offset = pl.multiple_of(p * LANES, LANES)

        def update(k, inner):
            mine = pl.ds(offset, LANES)
            pair = (hi_ref[k, mine, :], lo_ref[k, mine, :])
            work_ref[p] = work_ref[p] - product((hi_ref[k], lo_ref[k]), pair, NT)
            return inner

        lax.fori_loop(0, p, update, 0)
        inverse_factor(work_ref[p, pl.ds(offset, LANES), :], inverse_ref)
        solved = product(split(work_ref[p]), split(inverse_ref[...]), NT)
        hi_ref[p], lo_ref[p] = split(solved)
        work_ref[p] = solved
        return carry

    lax.fori_loop(0, panels, panel, 0)
    for p in range(panels):
        out_ref[:, p * LANES : (p + 1) * LANES] = work_ref[p, size:, :]


def any_orb_gram(part, top):
    halo = top.shape[0]
    current = jnp.concatenate([part[:halo] + top, part[halo:]], axis=0)
    rows = lax.all_to_all(current, "orb", split_axis=0, concat_axis=1, tiled=True)
    panels = rows.shape[1] // LANES
    packed = LANES * panels * (panels + 1) // 2
    gram = kernel_call(gram_kernel, f32(packed, LANES))(rows)
    dom = bits("dom")
    return rows, summed(gram, dom[:1] + bits("orb") + dom[1:]), packed_block


def two_orb_gram(part, top):
    own, cols = part.shape
    halo = top.shape[0]
    second = lax.axis_index("orb")
    panels = cols // LANES
    packed = LANES * (panels * (panels + 1) // 2 + panels * (panels // 2))
    flag = second.reshape(1)
    low = exchanged(part[halo:], "orb", 1)
    gram = low_gram(flag, part, low, halo, packed)
    high = exchanged(part[:halo] + top, "orb", 1)
    gram = high_gram(flag, part, top, high, gram)
    dom = bits("dom")
    stages = dom if len(dom) < 4 else dom[:-2] + [("dom", dom[-2][1], 4)]
    gram = scattered(gram, stages)
    for stage in reversed(stages[1:]):
        gram = gathered(gram, stage).reshape(-1, LANES)
    gram = gathered(gathered(gram, ("orb", 1, 2)), stages[0])
    mine = jnp.concatenate([part[:halo] + top, part[halo:]], axis=0).reshape(2, own // 2, cols)
    other = jnp.concatenate([high, low], axis=0).reshape(2, own // 2, cols)
    mine = jnp.where(second == 0, mine[0], mine[1])
    other = jnp.where(second == 0, other[0], other[1])
    rows = jnp.where(
        second == 0, jnp.concatenate([mine, other], axis=1), jnp.concatenate([other, mine], axis=1)
    )
    return rows, gram, halved_block


def with_flag(body, out_shape, count):
    specs = [pl.BlockSpec(memory_space=pltpu.SMEM)] + [pl.BlockSpec(memory_space=pltpu.VMEM)] * count
    return pl.pallas_call(
        body,
        out_shape=out_shape,
        in_specs=specs,
        compiler_params=pltpu.CompilerParams(vmem_limit_bytes=VMEM_BYTES),
    )


def low_gram(flag, part, low, halo, packed):
    kernel = lambda *refs: low_gram_kernel(halo, *refs)
    return with_flag(kernel, f32(packed, LANES), 2)(flag, part, low)


def high_gram(flag, part, top, high, gram):
    return with_flag(high_gram_kernel, f32(*gram.shape), 4)(flag, part, top, high, gram)


def body(orbitals, cell_mats, cell_map):
    own, cols = orbitals.shape
    size = cell_mats.shape[1]
    node_total = own * lax.axis_size("dom")
    matrix = kernel_call(order_kernel, [bf16(size, size)] * 2)(cell_map, cell_mats)
    part, top = filtered_columns(orbitals, matrix)
    two = lax.axis_size("orb") == 2 and cols % (2 * LANES) == 0 and lax.axis_size("dom") > 1
    rows, gram, block_of = (two_orb_gram if two else any_orb_gram)(part, top)
    count, width = rows.shape
    panels = width // LANES
    scratch = [
        pltpu.VMEM((panels, width + count, LANES), F32),
        pltpu.VMEM((panels, width + count, LANES), BF16),
        pltpu.VMEM((panels, width + count, LANES), BF16),
        pltpu.VMEM((LANES, LANES), F32),
    ]
    factor = lambda *refs: factor_kernel(1.0 / node_total, block_of, *refs)
    return kernel_call(factor, f32(count, width), scratch)(gram, rows)


def solution(mesh):
    placed = (P("dom", "orb"), P("dom", None, None), P("dom", None))
    return jax.shard_map(
        body, mesh=mesh, in_specs=placed, out_specs=P(("dom", "orb"), None), check_vma=False
    )
```

```python
import jax
import jax.numpy as jnp
from jax import lax
from jax.experimental import pallas as pl
from jax.experimental.pallas import tpu as pltpu
from jax.sharding import PartitionSpec as P

DEGREE = 5

filter_center = 2.0
filter_half = 3.5

F32, BF16 = jnp.float32, jnp.bfloat16
LANES, SUB = 128, 8
VMEM_BYTES = 48 << 20


def kernel_call(body, out_shape, scratch=()):
    return pl.pallas_call(
        body,
        out_shape=out_shape,
        scratch_shapes=list(scratch),
        compiler_params=pltpu.CompilerParams(vmem_limit_bytes=VMEM_BYTES),
    )


def f32(*shape):
    return jax.ShapeDtypeStruct(shape, F32)


def bf16(*shape):
    return jax.ShapeDtypeStruct(shape, BF16)


def split(v):
    hi = v.astype(BF16)
    return hi, (v - hi.astype(F32)).astype(BF16)


def contract(a, b, dims):
    return lax.dot_general(a, b, (dims, ((), ())), preferred_element_type=F32)


def product(a, b, dims):
    (a_hi, a_lo), (b_hi, b_lo) = a, b
    return contract(a_hi, b_hi, dims) + (contract(a_hi, b_lo, dims) + contract(a_lo, b_hi, dims))


NN = ((1,), (0,))
NT = ((1,), (1,))


def order_kernel(map_ref, cell_ref, hi_ref, lo_ref):
    size = cell_ref.shape[1]
    node = lax.broadcasted_iota(jnp.int32, (size, size), 0)
    pick = jnp.where(node == map_ref[...], 1.0, 0.0).astype(BF16)
    for half, out_ref in zip(split(cell_ref[0]), (hi_ref, lo_ref)):
        rows = contract(pick, half, NN).astype(BF16)
        out_ref[...] = contract(rows, pick, NT).astype(BF16)


def step_kernel(order, own, hi_ref, lo_ref, *refs):
    size = hi_ref.shape[0]
    halo = size - own
    if order == 0:
        own_ref, bottom_ref = refs[:2]
        vec = jnp.concatenate([own_ref[...], bottom_ref[...]], axis=0)
        outs = refs[2:]
    else:
        part_ref, top_ref, bottom_ref = refs[:3]
        vec = jnp.concatenate(
            [
                part_ref[:halo, :] + top_ref[...],
                part_ref[halo:own, :],
                part_ref[own:, :] + bottom_ref[...],
            ],
            axis=0,
        )
        outs = refs[3:]
    if order > 0:
        before_ref, outs = outs[0], outs[1:]
    scale = (1.0 if order == 0 else 2.0) / filter_half
    applied = product((hi_ref[...], lo_ref[...]), split(vec), NN) * scale
    part = applied - (filter_center * scale) * vec
    if order > 0:
        part = part - before_ref[...]
    if order == DEGREE - 1:
        next_ref, down_ref = outs
        next_ref[...] = part[:own]
    else:
        now_ref, next_ref, up_ref, down_ref = outs
        now_ref[...] = vec
        next_ref[...] = part
        up_ref[...] = applied[:halo]
    down_ref[...] = applied[own:]


def shifted(block, axis, distance):
    count = lax.axis_size(axis)
    route = [((i - distance) % count, i) for i in range(count)]
    return lax.ppermute(block, axis, route)


def filtered_columns(orbitals, matrix):
    own, cols = orbitals.shape
    size = matrix[0].shape[0]
    halo = size - own
    bottom = shifted(orbitals[:halo], "dom", -1)
    state = (orbitals, bottom)
    for order in range(DEGREE):
        last = order == DEGREE - 1
        outs = [f32(own if last else size, cols)]
        if not last:
            outs = [f32(size, cols)] + outs + [f32(halo, cols)]
        outs.append(f32(halo, cols))
        body = lambda *refs, order=order: step_kernel(order, own, *refs)
        got = kernel_call(body, outs)(*matrix, *state)
        if last:
            part, down = got
            top = shifted(down, "dom", 1)
            return part, top
        now, part, up, down = got
        top = shifted(down, "dom", 1)
        bottom = shifted(up, "dom", -1)
        state = (part, top, bottom, now)


def gram_kernel(rows_ref, out_ref):
    hi, lo = split(rows_ref[...].T)
    panels = hi.shape[0] // LANES
    at = 0
    for p in range(panels):
        cut = slice(p * LANES, (p + 1) * LANES)
        below = hi.shape[0] - p * LANES
        out_ref[at : at + below, :] = product((hi[p * LANES :], lo[p * LANES :]), (hi[cut], lo[cut]), NT)
        at += below


def half_gram(mine, other, second, out_ref, base_ref):
    own, own_lo = split(mine.T)
    other, other_lo = split(other.T)
    cols = own.shape[0]
    half = cols // 2

    def put(at, value):
        span = slice(at, at + value.shape[0])
        out_ref[span, :] = value if base_ref is None else base_ref[span, :] + value

    at = 0
    for p in range(0, cols, LANES):
        put(at, product((own[p:], own_lo[p:]), (own[p : p + LANES], own_lo[p : p + LANES]), NT))
        at += cols - p

    def cross(left, right):
        for i, p in enumerate(range(0, cols, LANES)):
            cut = slice(p, p + LANES)
            put(at + i * half, product(left, (right[0][cut], right[1][cut]), NT))

    @pl.when(second == 0)
    def _():
        cross((other[:half], other_lo[:half]), (own, own_lo))

    @pl.when(second == 1)
    def _():
        cross((own[half:], own_lo[half:]), (other, other_lo))


def low_gram_kernel(halo, second_ref, mine_ref, other_ref, out_ref):
    half_gram(mine_ref[halo:, :], other_ref[...], second_ref[0], out_ref, None)


def high_gram_kernel(pieces, second_ref, part_ref, top_ref, other_ref, base_ref, out_ref, all_ref):
    halo = top_ref.shape[0]
    half_gram(part_ref[:halo, :] + top_ref[...], other_ref[...], second_ref[0], all_ref, base_ref)
    panels = top_ref.shape[1] // LANES
    total = all_ref.shape[0]
    cut = LANES * panels * (panels + 1) // 2
    a, b, piece = cut // pieces, (total - cut) // pieces, total // pieces
    for i in range(pieces):
        out_ref[i * piece : i * piece + a, :] = all_ref[i * a : (i + 1) * a, :]
        out_ref[i * piece + a : (i + 1) * piece, :] = all_ref[cut + i * b : cut + (i + 1) * b, :]


def exchanged(block, axis, mask):
    route = [(i, i ^ mask) for i in range(lax.axis_size(axis))]
    return lax.ppermute(block, axis, route)


def bits(axis):
    count = lax.axis_size(axis)
    return [(axis, 1 << i, 2) for i in range(count.bit_length() - 1)]


def rank(axis, unit, count):
    return (lax.axis_index(axis) // unit) % count


def scattered(block, stages):
    for axis, unit, count in stages:
        mine = rank(axis, unit, count)
        pieces = block.reshape(count, -1, block.shape[-1])
        total = lax.dynamic_index_in_dim(pieces, mine, keepdims=False)
        for d in range(1, count):
            piece = lax.dynamic_index_in_dim(pieces, mine ^ d, keepdims=False)
            total = total + exchanged(piece, axis, d * unit)
        block = total
    return block


def gathered(block, stage):
    axis, unit, count = stage
    mine = rank(axis, unit, count)
    pieces = jnp.stack([block] + [exchanged(block, axis, d * unit) for d in range(1, count)])
    bit = 1
    while bit < count:
        pair = pieces.reshape((count // (2 * bit), 2, bit) + block.shape)
        pieces = jnp.where((mine & bit) != 0, pair[:, ::-1], pair).reshape(pieces.shape)
        bit *= 2
    return pieces


def summed(block, stages):
    width = block.shape[-1]
    block = scattered(block, stages)
    for stage in reversed(stages):
        block = gathered(block, stage).reshape(-1, width)
    return block


def inverse_factor(block, out_ref):
    size = block.shape[0]
    count = size // SUB
    shape = (SUB, size)
    rows = [block[t : t + SUB] for t in range(0, size, SUB)]
    sub = lax.broadcasted_iota(jnp.int32, shape, 0)
    lane = lax.broadcasted_iota(jnp.int32, shape, 1)

    def across(v, at):
        return [jnp.broadcast_to(v[:, at + k : at + k + 1], shape) for k in range(SUB)]

    def down(v, k):
        return jnp.broadcast_to(v[k : k + 1], shape)

    cols, below, ahead = across(rows[0], 0), across(rows[1], 0), across(rows[1], SUB)
    for b in range(count):
        at = b * SUB
        more = b + 1 < count
        raw = list(below)
        here = (lane >= at) & (lane < at + SUB)
        top = jnp.where(here, jnp.where(lane - at == sub, 1.0, 0.0), rows[b])
        scale = jnp.zeros(shape, F32)
        done = jnp.zeros(shape, F32)
        pivot = down(cols[0], 0)
        for k in range(SUB):
            inverse = 1.0 / pivot
            row = down(top, k)
            done = jnp.where(sub == k, row * lax.rsqrt(pivot), done)
            scale = jnp.where(sub == k, inverse, scale)
            heads = [down(cols[m], k) for m in range(k + 1, SUB)]
            if heads:
                pivot = down(cols[k + 1], k + 1) - (heads[0] * inverse) * heads[0]
            ratio = jnp.where(sub == k, 0.0, cols[k] * inverse)
            top = top - ratio * row
            part = below[k] * inverse
            for m, head in enumerate(heads, k + 1):
                cols[m] = cols[m] - ratio * head
                if more:
                    below[m] = below[m] - part * head
            if more:
                for j in range(SUB):
                    ahead[j] = ahead[j] - part * down(below[k], j)
        out_ref[at : at + SUB, :] = jnp.where(lane < at + SUB, done, 0.0)
        top = top * scale
        spread = [down(top, k) for k in range(SUB)]
        for t in range(b + 1, count):
            kept = jnp.where(here, 0.0, rows[t])
            for k, column in enumerate(raw if t == b + 1 else across(rows[t], at)):
                kept = kept - column * spread[k]
            rows[t] = kept
        cols = ahead
        if b + 2 < count:
            below, ahead = across(rows[b + 2], at + SUB), across(rows[b + 2], at + 2 * SUB)


def pair_of(v):
    return jnp.concatenate(split(v), axis=1)


def weights(pair):
    hi, lo = pair[:, :LANES], pair[:, LANES:]
    return jnp.concatenate(
        [jnp.concatenate([hi, hi], axis=1), jnp.concatenate([lo, jnp.zeros_like(lo)], axis=1)], axis=0
    )


def folded(pair, weight):
    both = contract(pair, weight, NT)
    half = both.shape[1] // 2
    return both[:, :half] + both[:, half:]


def factor_panels(work_ref, pair_ref, weight_ref, inverse_ref):
    def panel(p, carry):
        mine = pl.ds(pl.multiple_of(p * LANES, LANES), LANES)

        def update(k, inner):
            work_ref[p] = work_ref[p] - folded(pair_ref[k], weights(pair_ref[k, mine, :]))
            return inner

        lax.fori_loop(0, p, update, 0)
        inverse_factor(work_ref[p, mine, :], inverse_ref)
        weight = weights(pair_of(inverse_ref[...]))
        solved = folded(pair_of(work_ref[p]), weight)
        weight_ref[p] = weight
        pair_ref[p] = pair_of(solved)
        work_ref[p] = solved
        return carry

    lax.fori_loop(0, work_ref.shape[0], panel, 0)


def packed_block(gram_ref, row, col, panels):
    at = sum(panels - p for p in range(col)) + row - col
    return gram_ref[at * LANES : (at + 1) * LANES, :]


def factor_kernel(scale, gram_ref, rows_ref, out_ref, work_ref, pair_ref, weight_ref, inverse_ref):
    panels = work_ref.shape[0]
    size = panels * LANES
    for p in range(panels):
        for r in range(panels):
            block = packed_block(gram_ref, r, p, panels) * scale if r >= p else jnp.zeros((LANES, LANES), F32)
            work_ref[p, r * LANES : (r + 1) * LANES, :] = block
        work_ref[p, size:, :] = rows_ref[:, p * LANES : (p + 1) * LANES]
    factor_panels(work_ref, pair_ref, weight_ref, inverse_ref)
    for p in range(panels):
        out_ref[:, p * LANES : (p + 1) * LANES] = work_ref[p, size:, :]


def factor_all(gram, rows, scale):
    count, width = rows.shape
    panels = width // LANES
    scratch = [
        pltpu.VMEM((panels, width + count, LANES), F32),
        pltpu.VMEM((panels, width + count, 2 * LANES), BF16),
        pltpu.VMEM((panels, 2 * LANES, 2 * LANES), BF16),
        pltpu.VMEM((LANES, LANES), F32),
    ]
    return kernel_call(lambda *refs: factor_kernel(scale, *refs), f32(count, width), scratch)(gram, rows)


def quarter_block(ref, second, at):
    part, at = divmod(at, ref.shape[2] // LANES)
    return ref[part, second, at * LANES : (at + 1) * LANES, :]


def triangle_block(ref, second, row, col, panels):
    return quarter_block(ref, second, sum(panels - p for p in range(col)) + row - col)


def first_kernel(scale, tri_ref, rows_ref, out_ref, pair_ref, weight_ref, work_ref, inverse_ref):
    panels = work_ref.shape[0]
    size = panels * LANES
    for p in range(panels):
        for r in range(panels):
            block = jnp.zeros((LANES, LANES), F32)
            if r >= p:
                block = triangle_block(tri_ref, 0, r, p, panels) * scale
            work_ref[p, r * LANES : (r + 1) * LANES, :] = block
        work_ref[p, size:, :] = rows_ref[:, p * LANES : (p + 1) * LANES]
    factor_panels(work_ref, pair_ref, weight_ref, inverse_ref)
    for p in range(panels):
        out_ref[:, p * LANES : (p + 1) * LANES] = work_ref[p, size:, :]


def second_kernel(
    scale, tri_ref, cross_ref, rows_ref, done_ref, pair_ref, weight_ref,
    out_ref, work_ref, left_ref, new_pair_ref, new_weight_ref, inverse_ref,
):
    panels = work_ref.shape[0]
    size = panels * LANES
    half = panels // 2
    for p in range(panels):
        blocks = []
        for r in range(panels):
            second, inner = divmod(r, half)
            blocks.append(quarter_block(cross_ref, second, p * half + inner))
        solve = jnp.concatenate(blocks, axis=0) * scale
        for k in range(p):
            pair = left_ref[:size, 2 * k * LANES : 2 * (k + 1) * LANES]
            solve = solve - folded(pair, weights(pair_ref[k, p * LANES : (p + 1) * LANES, :]))
        span = slice(2 * p * LANES, 2 * (p + 1) * LANES)
        left_ref[:size, span] = pair_of(folded(pair_of(solve), weight_ref[p]))
        left_ref[size:, span] = pair_ref[p, size:, :]
    for p in range(panels):
        mine = left_ref[p * LANES : (p + 1) * LANES, :]
        weight = jnp.concatenate(
            [weights(mine[:, 2 * k * LANES : 2 * (k + 1) * LANES]) for k in range(panels)], axis=1
        )
        drop = folded(left_ref[...], weight)
        for r in range(panels):
            block = jnp.zeros((LANES, LANES), F32)
            if r >= p:
                block = triangle_block(tri_ref, 1, r, p, panels) * scale - drop[r * LANES : (r + 1) * LANES]
            work_ref[p, r * LANES : (r + 1) * LANES, :] = block
        work_ref[p, size:, :] = rows_ref[:, size + p * LANES : size + (p + 1) * LANES] - drop[size:]
    factor_panels(work_ref, new_pair_ref, new_weight_ref, inverse_ref)
    out_ref[:, :size] = done_ref[...]
    for p in range(panels):
        out_ref[:, size + p * LANES : size + (p + 1) * LANES] = work_ref[p, size:, :]


def factor_halves(tri, cross, rows, scale):
    count, width = rows.shape
    size = width // 2
    panels = size // LANES
    total = size + count
    pairs, weight = (panels, total, 2 * LANES), (panels, 2 * LANES, 2 * LANES)
    work = [pltpu.VMEM((panels, total, LANES), F32)]
    inverse = [pltpu.VMEM((LANES, LANES), F32)]
    done, pair, mult = kernel_call(
        lambda *refs: first_kernel(scale, *refs),
        [f32(count, size), bf16(*pairs), bf16(*weight)],
        work + inverse,
    )(tri, rows)
    more = [pltpu.VMEM((total, panels * 2 * LANES), BF16), pltpu.VMEM(pairs, BF16), pltpu.VMEM(weight, BF16)]
    return kernel_call(
        lambda *refs: second_kernel(scale, *refs), f32(count, width), work + more + inverse
    )(tri, cross, rows, done, pair, mult)


def any_orb(part, top, scale):
    halo = top.shape[0]
    current = jnp.concatenate([part[:halo] + top, part[halo:]], axis=0)
    rows = lax.all_to_all(current, "orb", split_axis=0, concat_axis=1, tiled=True)
    panels = rows.shape[1] // LANES
    packed = LANES * panels * (panels + 1) // 2
    gram = kernel_call(gram_kernel, f32(packed, LANES))(rows)
    dom = bits("dom")
    return factor_all(summed(gram, dom[:1] + bits("orb") + dom[1:]), rows, scale)


def two_orb(part, top, scale):
    own, cols = part.shape
    halo = top.shape[0]
    second = lax.axis_index("orb")
    panels = cols // LANES
    packed = LANES * (panels * (panels + 1) // 2 + panels * (panels // 2))
    flag = second.reshape(1)
    low = exchanged(part[halo:], "orb", 1)
    gram = low_gram(flag, part, low, halo, packed)
    high = exchanged(part[:halo] + top, "orb", 1)
    gram = high_gram(flag, part, top, high, gram)
    dom = bits("dom")
    stages = dom if len(dom) < 4 else dom[:-2] + [("dom", dom[-2][1], 4)]
    gram = scattered(gram, stages)
    cut = LANES * panels * (panels + 1) // 2 // lax.axis_size("dom")
    tri, cross = [everywhere(piece, stages) for piece in (gram[:cut], gram[cut:])]
    mine = jnp.concatenate([part[:halo] + top, part[halo:]], axis=0).reshape(2, own // 2, cols)
    other = jnp.concatenate([high, low], axis=0).reshape(2, own // 2, cols)
    mine = jnp.where(second == 0, mine[0], mine[1])
    other = jnp.where(second == 0, other[0], other[1])
    rows = jnp.where(
        second == 0, jnp.concatenate([mine, other], axis=1), jnp.concatenate([other, mine], axis=1)
    )
    return factor_halves(tri, cross, rows, scale)


def everywhere(block, stages):
    for stage in reversed(stages[1:]):
        block = gathered(block, stage).reshape(-1, LANES)
    return gathered(gathered(block, ("orb", 1, 2)), stages[0])


def with_flag(body, out_shape, count, scratch=()):
    specs = [pl.BlockSpec(memory_space=pltpu.SMEM)] + [pl.BlockSpec(memory_space=pltpu.VMEM)] * count
    return pl.pallas_call(
        body,
        out_shape=out_shape,
        in_specs=specs,
        scratch_shapes=list(scratch),
        compiler_params=pltpu.CompilerParams(vmem_limit_bytes=VMEM_BYTES),
    )


def low_gram(flag, part, low, halo, packed):
    kernel = lambda *refs: low_gram_kernel(halo, *refs)
    return with_flag(kernel, f32(packed, LANES), 2)(flag, part, low)


def high_gram(flag, part, top, high, gram):
    kernel = lambda *refs: high_gram_kernel(lax.axis_size("dom"), *refs)
    return with_flag(kernel, f32(*gram.shape), 4, [pltpu.VMEM(gram.shape, F32)])(flag, part, top, high, gram)


def body(orbitals, cell_mats, cell_map):
    own, cols = orbitals.shape
    size = cell_mats.shape[1]
    node_total = own * lax.axis_size("dom")
    matrix = kernel_call(order_kernel, [bf16(size, size)] * 2)(cell_map, cell_mats)
    part, top = filtered_columns(orbitals, matrix)
    panels = cols // LANES
    two = (
        lax.axis_size("orb") == 2
        and lax.axis_size("dom") > 1
        and cols % (2 * LANES) == 0
        and (LANES * panels * (panels + 1) // 2) % lax.axis_size("dom") == 0
        and (LANES * panels * panels // 2) % lax.axis_size("dom") == 0
    )
    return (two_orb if two else any_orb)(part, top, 1.0 / node_total)


def solution(mesh):
    placed = (P("dom", "orb"), P("dom", None, None), P("dom", None))
    return jax.shard_map(
        body, mesh=mesh, in_specs=placed, out_specs=P(("dom", "orb"), None), check_vma=False
    )
```

```python
import jax
import jax.numpy as jnp
from jax import lax
from jax.experimental import pallas as pl
from jax.experimental.pallas import tpu as pltpu
from jax.sharding import PartitionSpec as P

DEGREE = 5

filter_center = 2.0
filter_half = 3.5

F32, BF16 = jnp.float32, jnp.bfloat16
LANES, SUB = 128, 8
VMEM_BYTES = 24 << 20


def kernel_call(body, out_shape, scratch=()):
    return pl.pallas_call(
        body,
        out_shape=out_shape,
        scratch_shapes=list(scratch),
        compiler_params=pltpu.CompilerParams(vmem_limit_bytes=VMEM_BYTES),
    )


def f32(*shape):
    return jax.ShapeDtypeStruct(shape, F32)


def bf16(*shape):
    return jax.ShapeDtypeStruct(shape, BF16)


def split(v):
    hi = v.astype(BF16)
    return hi, (v - hi.astype(F32)).astype(BF16)


def contract(a, b, dims):
    return lax.dot_general(a, b, (dims, ((), ())), preferred_element_type=F32)


def product(a, b, dims):
    (a_hi, a_lo), (b_hi, b_lo) = a, b
    return contract(a_hi, b_hi, dims) + (contract(a_hi, b_lo, dims) + contract(a_lo, b_hi, dims))


NN = ((1,), (0,))
NT = ((1,), (1,))


def order_kernel(map_ref, cell_ref, hi_ref, lo_ref):
    size = cell_ref.shape[1]
    node = lax.broadcasted_iota(jnp.int32, (size, size), 0)
    pick = jnp.where(node == map_ref[...], 1.0, 0.0).astype(BF16)
    for half, out_ref in zip(split(cell_ref[0]), (hi_ref, lo_ref)):
        rows = contract(pick, half, NN).astype(BF16)
        out_ref[...] = contract(rows, pick, NT).astype(BF16)


def first_kernel_of_filter(hi_ref, lo_ref, own_ref, applied_ref):
    own = own_ref.shape[0]
    scale = 1.0 / filter_half
    applied_ref[...] = product((hi_ref[:, :own], lo_ref[:, :own]), split(own_ref[...]), NN) * scale


def edge_columns(ref, own, first, rows=slice(None)):
    right = ref[rows, own:]
    if first:
        return right
    return jnp.concatenate([ref[rows, : ref.shape[1] - own], right], axis=1)


def edge_kernel(order, own, hi_ref, lo_ref, applied_ref, *refs):
    halo = hi_ref.shape[0] - own
    scale = (1.0 if order == 0 else 2.0) / filter_half
    count = 1 if order == 0 else 2
    delta = split(jnp.concatenate([ref[...] for ref in refs[:count]], axis=0))
    outs = refs[count:]
    spans = [slice(own, own + halo)] if order == DEGREE - 1 else [slice(0, halo), slice(own, own + halo)]
    for span, out_ref in zip(spans, outs):
        block = [edge_columns(ref, own, order == 0, span) for ref in (hi_ref, lo_ref)]
        out_ref[...] = applied_ref[span, :] + product(block, delta, NN) * scale


def rest_kernel(order, own, hi_ref, lo_ref, applied_ref, vec_ref, *refs):
    halo = hi_ref.shape[0] - own
    scale = (1.0 if order == 0 else 2.0) / filter_half
    last = order == DEGREE - 1
    if order == 0:
        bottom = refs[0][...]
        delta, outs = bottom, refs[1:]
        vec = jnp.concatenate([vec_ref[...], bottom], axis=0)
    else:
        top, bottom, before_ref = refs[0][...], refs[1][...], refs[2]
        delta, outs = jnp.concatenate([top, bottom], axis=0), refs[3:]
        vec = jnp.concatenate(
            [vec_ref[:halo, :] + top, vec_ref[halo:own, :], vec_ref[own:, :] + bottom], axis=0
        )
    rows = slice(0, own) if last else slice(0, own + halo)
    columns = [edge_columns(ref, own, order == 0, rows) for ref in (hi_ref, lo_ref)]
    part = applied_ref[rows, :] + product(columns, split(delta), NN) * scale
    part = part - (filter_center * scale) * vec[rows]
    if order > 0:
        part = part - before_ref[rows, :]
    outs[0][...] = part
    if not last:
        outs[1][...] = vec
        outs[2][...] = product((hi_ref[...], lo_ref[...]), split(part), NN) * (2.0 / filter_half)


def shifted(block, axis, distance):
    count = lax.axis_size(axis)
    route = [((i - distance) % count, i) for i in range(count)]
    return lax.ppermute(block, axis, route)


def filtered_columns(orbitals, matrix):
    own, cols = orbitals.shape
    size = matrix[0].shape[0]
    halo = size - own
    arrived = (shifted(orbitals[:halo], "dom", -1),)
    applied = kernel_call(first_kernel_of_filter, f32(size, cols))(*matrix, orbitals)
    vec, before = orbitals, ()
    for order in range(DEGREE):
        last = order == DEGREE - 1
        edge = lambda *refs, order=order: edge_kernel(order, own, *refs)
        rest = lambda *refs, order=order: rest_kernel(order, own, *refs)
        sent = kernel_call(edge, [f32(halo, cols)] * (1 if last else 2))(*matrix, applied, *arrived)
        moved = [shifted(sent[-1], "dom", 1)]
        if not last:
            moved.append(shifted(sent[0], "dom", -1))
        outs = [f32(own, cols)] if last else [f32(size, cols)] * 3
        got = kernel_call(rest, outs)(*matrix, applied, vec, *arrived, *before)
        if last:
            return got[0], moved[0]
        vec, before, applied = got[0], (got[1],), got[2]
        arrived = tuple(moved)


def gram_kernel(rows_ref, out_ref):
    hi, lo = split(rows_ref[...].T)
    panels = hi.shape[0] // LANES
    at = 0
    for p in range(panels):
        cut = slice(p * LANES, (p + 1) * LANES)
        below = hi.shape[0] - p * LANES
        out_ref[at : at + below, :] = product((hi[p * LANES :], lo[p * LANES :]), (hi[cut], lo[cut]), NT)
        at += below


def half_gram(mine, other, second, out_ref, base_ref):
    own, own_lo = split(mine.T)
    other, other_lo = split(other.T)
    cols = own.shape[0]
    half = cols // 2

    def put(at, value):
        span = slice(at, at + value.shape[0])
        out_ref[span, :] = value if base_ref is None else base_ref[span, :] + value

    at = 0
    for p in range(0, cols, LANES):
        put(at, product((own[p:], own_lo[p:]), (own[p : p + LANES], own_lo[p : p + LANES]), NT))
        at += cols - p

    def cross(left, right):
        for i, p in enumerate(range(0, cols, LANES)):
            cut = slice(p, p + LANES)
            put(at + i * half, product(left, (right[0][cut], right[1][cut]), NT))

    @pl.when(second == 0)
    def _():
        cross((other[:half], other_lo[:half]), (own, own_lo))

    @pl.when(second == 1)
    def _():
        cross((own[half:], own_lo[half:]), (other, other_lo))


def low_gram_kernel(halo, second_ref, mine_ref, other_ref, out_ref):
    half_gram(mine_ref[halo:, :], other_ref[...], second_ref[0], out_ref, None)


def high_gram_kernel(pieces, second_ref, part_ref, top_ref, other_ref, base_ref, out_ref, all_ref):
    halo = top_ref.shape[0]
    half_gram(part_ref[:halo, :] + top_ref[...], other_ref[...], second_ref[0], all_ref, base_ref)
    panels = top_ref.shape[1] // LANES
    total = all_ref.shape[0]
    cut = LANES * panels * (panels + 1) // 2
    a, b, piece = cut // pieces, (total - cut) // pieces, total // pieces
    for i in range(pieces):
        out_ref[i * piece : i * piece + a, :] = all_ref[i * a : (i + 1) * a, :]
        out_ref[i * piece + a : (i + 1) * piece, :] = all_ref[cut + i * b : cut + (i + 1) * b, :]


def exchanged(block, axis, mask):
    route = [(i, i ^ mask) for i in range(lax.axis_size(axis))]
    return lax.ppermute(block, axis, route)


def bits(axis):
    count = lax.axis_size(axis)
    return [(axis, 1 << i, 2) for i in range(count.bit_length() - 1)]


def rank(axis, unit, count):
    return (lax.axis_index(axis) // unit) % count


def scattered(block, stages):
    for axis, unit, count in stages:
        mine = rank(axis, unit, count)
        pieces = block.reshape(count, -1, block.shape[-1])
        total = lax.dynamic_index_in_dim(pieces, mine, keepdims=False)
        for d in range(1, count):
            piece = lax.dynamic_index_in_dim(pieces, mine ^ d, keepdims=False)
            total = total + exchanged(piece, axis, d * unit)
        block = total
    return block


def gathered(block, stage):
    axis, unit, count = stage
    mine = rank(axis, unit, count)
    pieces = jnp.stack([block] + [exchanged(block, axis, d * unit) for d in range(1, count)])
    bit = 1
    while bit < count:
        pair = pieces.reshape((count // (2 * bit), 2, bit) + block.shape)
        pieces = jnp.where((mine & bit) != 0, pair[:, ::-1], pair).reshape(pieces.shape)
        bit *= 2
    return pieces


def summed(block, stages):
    width = block.shape[-1]
    block = scattered(block, stages)
    for stage in reversed(stages):
        block = gathered(block, stage).reshape(-1, width)
    return block


def inverse_factor(block, out_ref):
    size = block.shape[0]
    count = size // SUB
    shape = (SUB, size)
    rows = [block[t : t + SUB] for t in range(0, size, SUB)]
    sub = lax.broadcasted_iota(jnp.int32, shape, 0)
    lane = lax.broadcasted_iota(jnp.int32, shape, 1)

    def across(v, at):
        return [jnp.broadcast_to(v[:, at + k : at + k + 1], shape) for k in range(SUB)]

    def down(v, k):
        return jnp.broadcast_to(v[k : k + 1], shape)

    cols, below, ahead = across(rows[0], 0), across(rows[1], 0), across(rows[1], SUB)
    for b in range(count):
        at = b * SUB
        more = b + 1 < count
        raw = list(below)
        here = (lane >= at) & (lane < at + SUB)
        top = jnp.where(here, jnp.where(lane - at == sub, 1.0, 0.0), rows[b])
        scale = jnp.zeros(shape, F32)
        done = jnp.zeros(shape, F32)
        pivot = down(cols[0], 0)
        for k in range(SUB):
            inverse = 1.0 / pivot
            row = down(top, k)
            done = jnp.where(sub == k, row * lax.rsqrt(pivot), done)
            scale = jnp.where(sub == k, inverse, scale)
            heads = [down(cols[m], k) for m in range(k + 1, SUB)]
            if heads:
                pivot = down(cols[k + 1], k + 1) - (heads[0] * inverse) * heads[0]
            ratio = jnp.where(sub == k, 0.0, cols[k] * inverse)
            top = top - ratio * row
            part = below[k] * inverse
            for m, head in enumerate(heads, k + 1):
                cols[m] = cols[m] - ratio * head
                if more:
                    below[m] = below[m] - part * head
            if more:
                for j in range(SUB):
                    ahead[j] = ahead[j] - part * down(below[k], j)
        out_ref[at : at + SUB, :] = jnp.where(lane < at + SUB, done, 0.0)
        top = top * scale
        spread = [down(top, k) for k in range(SUB)]
        for t in range(b + 1, count):
            kept = jnp.where(here, 0.0, rows[t])
            for k, column in enumerate(raw if t == b + 1 else across(rows[t], at)):
                kept = kept - column * spread[k]
            rows[t] = kept
        cols = ahead
        if b + 2 < count:
            below, ahead = across(rows[b + 2], at + SUB), across(rows[b + 2], at + 2 * SUB)


def pair_of(v):
    return jnp.concatenate(split(v), axis=1)


def weights(pair):
    hi, lo = pair[:, :LANES], pair[:, LANES:]
    return jnp.concatenate(
        [jnp.concatenate([hi, hi], axis=1), jnp.concatenate([lo, jnp.zeros_like(lo)], axis=1)], axis=0
    )


def folded(pair, weight):
    both = contract(pair, weight, NT)
    half = both.shape[1] // 2
    return both[:, :half] + both[:, half:]


def factor_panels(work_ref, pair_ref, weight_ref, inverse_ref):
    def panel(p, carry):
        mine = pl.ds(pl.multiple_of(p * LANES, LANES), LANES)

        def update(k, inner):
            work_ref[p] = work_ref[p] - folded(pair_ref[k], weights(pair_ref[k, mine, :]))
            return inner

        lax.fori_loop(0, p, update, 0)
        inverse_factor(work_ref[p, mine, :], inverse_ref)
        weight = weights(pair_of(inverse_ref[...]))
        solved = folded(pair_of(work_ref[p]), weight)
        weight_ref[p] = weight
        pair_ref[p] = pair_of(solved)
        work_ref[p] = solved
        return carry

    lax.fori_loop(0, work_ref.shape[0], panel, 0)


def packed_block(gram_ref, row, col, panels):
    at = sum(panels - p for p in range(col)) + row - col
    return gram_ref[at * LANES : (at + 1) * LANES, :]


def factor_kernel(scale, gram_ref, rows_ref, out_ref, work_ref, pair_ref, weight_ref, inverse_ref):
    panels = work_ref.shape[0]
    size = panels * LANES
    for p in range(panels):
        for r in range(panels):
            block = packed_block(gram_ref, r, p, panels) * scale if r >= p else jnp.zeros((LANES, LANES), F32)
            work_ref[p, r * LANES : (r + 1) * LANES, :] = block
        work_ref[p, size:, :] = rows_ref[:, p * LANES : (p + 1) * LANES]
    factor_panels(work_ref, pair_ref, weight_ref, inverse_ref)
    for p in range(panels):
        out_ref[:, p * LANES : (p + 1) * LANES] = work_ref[p, size:, :]


def factor_all(gram, rows, scale):
    count, width = rows.shape
    panels = width // LANES
    scratch = [
        pltpu.VMEM((panels, width + count, LANES), F32),
        pltpu.VMEM((panels, width + count, 2 * LANES), BF16),
        pltpu.VMEM((panels, 2 * LANES, 2 * LANES), BF16),
        pltpu.VMEM((LANES, LANES), F32),
    ]
    return kernel_call(lambda *refs: factor_kernel(scale, *refs), f32(count, width), scratch)(gram, rows)


def quarter_block(ref, second, at):
    part, at = divmod(at, ref.shape[2] // LANES)
    return ref[part, second, at * LANES : (at + 1) * LANES, :]


def triangle_block(ref, second, row, col, panels):
    return quarter_block(ref, second, sum(panels - p for p in range(col)) + row - col)


def first_kernel(scale, tri_ref, rows_ref, out_ref, pair_ref, weight_ref, work_ref, inverse_ref):
    panels = work_ref.shape[0]
    size = panels * LANES
    for p in range(panels):
        for r in range(panels):
            block = jnp.zeros((LANES, LANES), F32)
            if r >= p:
                block = triangle_block(tri_ref, 0, r, p, panels) * scale
            work_ref[p, r * LANES : (r + 1) * LANES, :] = block
        work_ref[p, size:, :] = rows_ref[:, p * LANES : (p + 1) * LANES]
    factor_panels(work_ref, pair_ref, weight_ref, inverse_ref)
    for p in range(panels):
        out_ref[:, p * LANES : (p + 1) * LANES] = work_ref[p, size:, :]


def second_kernel(
    scale, tri_ref, cross_ref, rows_ref, done_ref, pair_ref, weight_ref,
    out_ref, work_ref, left_ref, new_pair_ref, new_weight_ref, inverse_ref,
):
    panels = work_ref.shape[0]
    size = panels * LANES
    half = panels // 2
    for p in range(panels):
        blocks = []
        for r in range(panels):
            second, inner = divmod(r, half)
            blocks.append(quarter_block(cross_ref, second, p * half + inner))
        solve = jnp.concatenate(blocks, axis=0) * scale
        for k in range(p):
            pair = left_ref[:size, 2 * k * LANES : 2 * (k + 1) * LANES]
            solve = solve - folded(pair, weights(pair_ref[k, p * LANES : (p + 1) * LANES, :]))
        span = slice(2 * p * LANES, 2 * (p + 1) * LANES)
        left_ref[:size, span] = pair_of(folded(pair_of(solve), weight_ref[p]))
        left_ref[size:, span] = pair_ref[p, size:, :]
    for p in range(panels):
        mine = left_ref[p * LANES : (p + 1) * LANES, :]
        weight = jnp.concatenate(
            [weights(mine[:, 2 * k * LANES : 2 * (k + 1) * LANES]) for k in range(panels)], axis=1
        )
        drop = folded(left_ref[...], weight)
        for r in range(panels):
            block = jnp.zeros((LANES, LANES), F32)
            if r >= p:
                block = triangle_block(tri_ref, 1, r, p, panels) * scale - drop[r * LANES : (r + 1) * LANES]
            work_ref[p, r * LANES : (r + 1) * LANES, :] = block
        work_ref[p, size:, :] = rows_ref[:, size + p * LANES : size + (p + 1) * LANES] - drop[size:]
    factor_panels(work_ref, new_pair_ref, new_weight_ref, inverse_ref)
    out_ref[:, :size] = done_ref[...]
    for p in range(panels):
        out_ref[:, size + p * LANES : size + (p + 1) * LANES] = work_ref[p, size:, :]


def factor_halves(tri, cross, rows, scale):
    count, width = rows.shape
    size = width // 2
    panels = size // LANES
    total = size + count
    pairs, weight = (panels, total, 2 * LANES), (panels, 2 * LANES, 2 * LANES)
    work = [pltpu.VMEM((panels, total, LANES), F32)]
    inverse = [pltpu.VMEM((LANES, LANES), F32)]
    done, pair, mult = kernel_call(
        lambda *refs: first_kernel(scale, *refs),
        [f32(count, size), bf16(*pairs), bf16(*weight)],
        work + inverse,
    )(tri, rows)
    more = [pltpu.VMEM((total, panels * 2 * LANES), BF16), pltpu.VMEM(pairs, BF16), pltpu.VMEM(weight, BF16)]
    return kernel_call(
        lambda *refs: second_kernel(scale, *refs), f32(count, width), work + more + inverse
    )(tri, cross, rows, done, pair, mult)


def any_orb(part, top, scale):
    halo = top.shape[0]
    current = jnp.concatenate([part[:halo] + top, part[halo:]], axis=0)
    rows = lax.all_to_all(current, "orb", split_axis=0, concat_axis=1, tiled=True)
    panels = rows.shape[1] // LANES
    packed = LANES * panels * (panels + 1) // 2
    gram = kernel_call(gram_kernel, f32(packed, LANES))(rows)
    dom = bits("dom")
    return factor_all(summed(gram, dom[:1] + bits("orb") + dom[1:]), rows, scale)


def two_orb(part, top, scale):
    own, cols = part.shape
    halo = top.shape[0]
    second = lax.axis_index("orb")
    panels = cols // LANES
    packed = LANES * (panels * (panels + 1) // 2 + panels * (panels // 2))
    flag = second.reshape(1)
    low = exchanged(part[halo:], "orb", 1)
    gram = low_gram(flag, part, low, halo, packed)
    high = exchanged(part[:halo] + top, "orb", 1)
    gram = high_gram(flag, part, top, high, gram)
    dom = bits("dom")
    stages = dom if len(dom) < 4 else dom[:-2] + [("dom", dom[-2][1], 4)]
    gram = scattered(gram, stages)
    cut = LANES * panels * (panels + 1) // 2 // lax.axis_size("dom")
    tri, cross = [everywhere(piece, stages) for piece in (gram[:cut], gram[cut:])]
    mine = jnp.concatenate([part[:halo] + top, part[halo:]], axis=0).reshape(2, own // 2, cols)
    other = jnp.concatenate([high, low], axis=0).reshape(2, own // 2, cols)
    mine = jnp.where(second == 0, mine[0], mine[1])
    other = jnp.where(second == 0, other[0], other[1])
    rows = jnp.where(
        second == 0, jnp.concatenate([mine, other], axis=1), jnp.concatenate([other, mine], axis=1)
    )
    return factor_halves(tri, cross, rows, scale)


def everywhere(block, stages):
    for stage in reversed(stages[1:]):
        block = gathered(block, stage).reshape(-1, LANES)
    return gathered(gathered(block, ("orb", 1, 2)), stages[0])


def with_flag(body, out_shape, count, scratch=()):
    specs = [pl.BlockSpec(memory_space=pltpu.SMEM)] + [pl.BlockSpec(memory_space=pltpu.VMEM)] * count
    return pl.pallas_call(
        body,
        out_shape=out_shape,
        in_specs=specs,
        scratch_shapes=list(scratch),
        compiler_params=pltpu.CompilerParams(vmem_limit_bytes=VMEM_BYTES),
    )


def low_gram(flag, part, low, halo, packed):
    kernel = lambda *refs: low_gram_kernel(halo, *refs)
    return with_flag(kernel, f32(packed, LANES), 2)(flag, part, low)


def high_gram(flag, part, top, high, gram):
    kernel = lambda *refs: high_gram_kernel(lax.axis_size("dom"), *refs)
    return with_flag(kernel, f32(*gram.shape), 4, [pltpu.VMEM(gram.shape, F32)])(flag, part, top, high, gram)


def body(orbitals, cell_mats, cell_map):
    own, cols = orbitals.shape
    size = cell_mats.shape[1]
    node_total = own * lax.axis_size("dom")
    matrix = kernel_call(order_kernel, [bf16(size, size)] * 2)(cell_map, cell_mats)
    part, top = filtered_columns(orbitals, matrix)
    panels = cols // LANES
    two = (
        lax.axis_size("orb") == 2
        and lax.axis_size("dom") > 1
        and cols % (2 * LANES) == 0
        and (LANES * panels * (panels + 1) // 2) % lax.axis_size("dom") == 0
        and (LANES * panels * panels // 2) % lax.axis_size("dom") == 0
    )
    return (two_orb if two else any_orb)(part, top, 1.0 / node_total)


def solution(mesh):
    placed = (P("dom", "orb"), P("dom", None, None), P("dom", None))
    return jax.shard_map(
        body, mesh=mesh, in_specs=placed, out_specs=P(("dom", "orb"), None), check_vma=False
    )
```

```python
import jax
import jax.numpy as jnp
from jax import lax
from jax.experimental import pallas as pl
from jax.experimental.pallas import tpu as pltpu
from jax.sharding import PartitionSpec as P

DEGREE = 5

filter_center = 2.0
filter_half = 3.5

F32, BF16 = jnp.float32, jnp.bfloat16
LANES, SUB = 128, 8
VMEM_BYTES = 24 << 20


def kernel_call(body, out_shape, scratch=()):
    return pl.pallas_call(
        body,
        out_shape=out_shape,
        scratch_shapes=list(scratch),
        compiler_params=pltpu.CompilerParams(vmem_limit_bytes=VMEM_BYTES),
    )


def f32(*shape):
    return jax.ShapeDtypeStruct(shape, F32)


def bf16(*shape):
    return jax.ShapeDtypeStruct(shape, BF16)


def split(v):
    hi = v.astype(BF16)
    return hi, (v - hi.astype(F32)).astype(BF16)


def contract(a, b, dims):
    return lax.dot_general(a, b, (dims, ((), ())), preferred_element_type=F32)


def product(a, b, dims):
    (a_hi, a_lo), (b_hi, b_lo) = a, b
    return contract(a_hi, b_hi, dims) + (contract(a_hi, b_lo, dims) + contract(a_lo, b_hi, dims))


NN = ((1,), (0,))
NT = ((1,), (1,))


def order_kernel(map_ref, cell_ref, hi_ref, lo_ref):
    size = cell_ref.shape[1]
    node = lax.broadcasted_iota(jnp.int32, (size, size), 0)
    pick = jnp.where(node == map_ref[...], 1.0, 0.0).astype(BF16)
    for half, out_ref in zip(split(cell_ref[0]), (hi_ref, lo_ref)):
        rows = contract(pick, half, NN).astype(BF16)
        out_ref[...] = contract(rows, pick, NT).astype(BF16)


def first_kernel_of_filter(hi_ref, lo_ref, own_ref, applied_ref):
    own = own_ref.shape[0]
    scale = 1.0 / filter_half
    applied_ref[...] = product((hi_ref[:, :own], lo_ref[:, :own]), split(own_ref[...]), NN) * scale


def edge_columns(ref, own, first, rows=slice(None)):
    right = ref[rows, own:]
    if first:
        return right
    return jnp.concatenate([ref[rows, : ref.shape[1] - own], right], axis=1)


def edge_kernel(order, own, hi_ref, lo_ref, applied_ref, *refs):
    halo = hi_ref.shape[0] - own
    scale = (1.0 if order == 0 else 2.0) / filter_half
    count = 1 if order == 0 else 2
    delta = split(jnp.concatenate([ref[...] for ref in refs[:count]], axis=0))
    outs = refs[count:]
    spans = [slice(own, own + halo)] if order == DEGREE - 1 else [slice(0, halo), slice(own, own + halo)]
    for span, out_ref in zip(spans, outs):
        block = [edge_columns(ref, own, order == 0, span) for ref in (hi_ref, lo_ref)]
        out_ref[...] = applied_ref[span, :] + product(block, delta, NN) * scale


def rest_kernel(order, own, hi_ref, lo_ref, applied_ref, vec_ref, *refs):
    halo = hi_ref.shape[0] - own
    scale = (1.0 if order == 0 else 2.0) / filter_half
    last = order == DEGREE - 1
    if order == 0:
        bottom = refs[0][...]
        delta, outs = bottom, refs[1:]
        vec = jnp.concatenate([vec_ref[...], bottom], axis=0)
    else:
        top, bottom, before_ref = refs[0][...], refs[1][...], refs[2]
        delta, outs = jnp.concatenate([top, bottom], axis=0), refs[3:]
        vec = jnp.concatenate(
            [vec_ref[:halo, :] + top, vec_ref[halo:own, :], vec_ref[own:, :] + bottom], axis=0
        )
    rows = slice(0, own) if last else slice(0, own + halo)
    columns = [edge_columns(ref, own, order == 0, rows) for ref in (hi_ref, lo_ref)]
    part = applied_ref[rows, :] + product(columns, split(delta), NN) * scale
    part = part - (filter_center * scale) * vec[rows]
    if order > 0:
        part = part - before_ref[rows, :]
    outs[0][...] = part
    if not last:
        outs[1][...] = vec
        outs[2][...] = product((hi_ref[...], lo_ref[...]), split(part), NN) * (2.0 / filter_half)


def shifted(block, axis, distance):
    count = lax.axis_size(axis)
    route = [((i - distance) % count, i) for i in range(count)]
    return lax.ppermute(block, axis, route)


def filtered_columns(orbitals, matrix):
    own, cols = orbitals.shape
    size = matrix[0].shape[0]
    halo = size - own
    arrived = (shifted(orbitals[:halo], "dom", -1),)
    applied = kernel_call(first_kernel_of_filter, f32(size, cols))(*matrix, orbitals)
    vec, before = orbitals, ()
    for order in range(DEGREE):
        last = order == DEGREE - 1
        edge = lambda *refs, order=order: edge_kernel(order, own, *refs)
        rest = lambda *refs, order=order: rest_kernel(order, own, *refs)
        sent = kernel_call(edge, [f32(halo, cols)] * (1 if last else 2))(*matrix, applied, *arrived)
        moved = [shifted(sent[-1], "dom", 1)]
        if not last:
            moved.append(shifted(sent[0], "dom", -1))
        outs = [f32(own, cols)] if last else [f32(size, cols)] * 3
        got = kernel_call(rest, outs)(*matrix, applied, vec, *arrived, *before)
        if last:
            return got[0], moved[0]
        vec, before, applied = got[0], (got[1],), got[2]
        arrived = tuple(moved)


def gram_kernel(rows_ref, out_ref):
    hi, lo = split(rows_ref[...].T)
    panels = hi.shape[0] // LANES
    at = 0
    for p in range(panels):
        cut = slice(p * LANES, (p + 1) * LANES)
        below = hi.shape[0] - p * LANES
        out_ref[at : at + below, :] = product((hi[p * LANES :], lo[p * LANES :]), (hi[cut], lo[cut]), NT)
        at += below


def half_gram(mine, other, second, out_ref, base_ref):
    own, own_lo = split(mine.T)
    other, other_lo = split(other.T)
    cols = own.shape[0]
    half = cols // 2

    def put(at, value):
        span = slice(at, at + value.shape[0])
        out_ref[span, :] = value if base_ref is None else base_ref[span, :] + value

    at = 0
    for p in range(0, cols, LANES):
        put(at, product((own[p:], own_lo[p:]), (own[p : p + LANES], own_lo[p : p + LANES]), NT))
        at += cols - p

    def cross(left, right):
        for i, p in enumerate(range(0, cols, LANES)):
            cut = slice(p, p + LANES)
            put(at + i * half, product(left, (right[0][cut], right[1][cut]), NT))

    @pl.when(second == 0)
    def _():
        cross((other[:half], other_lo[:half]), (own, own_lo))

    @pl.when(second == 1)
    def _():
        cross((own[half:], own_lo[half:]), (other, other_lo))


def low_gram_kernel(halo, second_ref, mine_ref, other_ref, out_ref):
    half_gram(mine_ref[halo:, :], other_ref[...], second_ref[0], out_ref, None)


def high_gram_kernel(pieces, second_ref, part_ref, top_ref, other_ref, base_ref, out_ref, all_ref):
    halo = top_ref.shape[0]
    half_gram(part_ref[:halo, :] + top_ref[...], other_ref[...], second_ref[0], all_ref, base_ref)
    panels = top_ref.shape[1] // LANES
    total = all_ref.shape[0]
    cut = LANES * panels * (panels + 1) // 2
    a, b, piece = cut // pieces, (total - cut) // pieces, total // pieces
    for i in range(pieces):
        out_ref[i * piece : i * piece + a, :] = all_ref[i * a : (i + 1) * a, :]
        out_ref[i * piece + a : (i + 1) * piece, :] = all_ref[cut + i * b : cut + (i + 1) * b, :]


def exchanged(block, axis, mask):
    route = [(i, i ^ mask) for i in range(lax.axis_size(axis))]
    return lax.ppermute(block, axis, route)


def bits(axis):
    count = lax.axis_size(axis)
    return [(axis, 1 << i, 2) for i in range(count.bit_length() - 1)]


def rank(axis, unit, count):
    return (lax.axis_index(axis) // unit) % count


def scattered(block, stages):
    for axis, unit, count in stages:
        mine = rank(axis, unit, count)
        pieces = block.reshape(count, -1, block.shape[-1])
        total = lax.dynamic_index_in_dim(pieces, mine, keepdims=False)
        for d in range(1, count):
            piece = lax.dynamic_index_in_dim(pieces, mine ^ d, keepdims=False)
            total = total + exchanged(piece, axis, d * unit)
        block = total
    return block


def gathered(block, stage):
    axis, unit, count = stage
    mine = rank(axis, unit, count)
    pieces = jnp.stack([block] + [exchanged(block, axis, d * unit) for d in range(1, count)])
    bit = 1
    while bit < count:
        pair = pieces.reshape((count // (2 * bit), 2, bit) + block.shape)
        pieces = jnp.where((mine & bit) != 0, pair[:, ::-1], pair).reshape(pieces.shape)
        bit *= 2
    return pieces


def summed(block, stages):
    width = block.shape[-1]
    block = scattered(block, stages)
    for stage in reversed(stages):
        block = gathered(block, stage).reshape(-1, width)
    return block


def inverse_factor(block, out_ref):
    size = block.shape[0]
    count = size // SUB
    shape = (SUB, size)
    rows = [block[t : t + SUB] for t in range(0, size, SUB)]
    sub = lax.broadcasted_iota(jnp.int32, shape, 0)
    lane = lax.broadcasted_iota(jnp.int32, shape, 1)

    def across(v, at):
        return [jnp.broadcast_to(v[:, at + k : at + k + 1], shape) for k in range(SUB)]

    def down(v, k):
        return jnp.broadcast_to(v[k : k + 1], shape)

    for start in range(0, count, count // 2):
        stop, at = start + count // 2, start * SUB
        cols, below = across(rows[start], at), across(rows[start + 1], at)
        ahead = across(rows[start + 1], at + SUB)
        near = []
        for b in range(start, stop):
            at = b * SUB
            more = b + 1 < stop
            raw = list(below)
            here = (lane >= at) & (lane < at + SUB)
            top = jnp.where(here, jnp.where(lane - at == sub, 1.0, 0.0), rows[b])
            scale = jnp.zeros(shape, F32)
            done = jnp.zeros(shape, F32)
            pivot = down(cols[0], 0)
            for k in range(SUB):
                inverse = 1.0 / pivot
                row = down(top, k)
                done = jnp.where(sub == k, row * lax.rsqrt(pivot), done)
                scale = jnp.where(sub == k, inverse, scale)
                heads = [down(cols[m], k) for m in range(k + 1, SUB)]
                if heads:
                    pivot = down(cols[k + 1], k + 1) - (heads[0] * inverse) * heads[0]
                ratio = jnp.where(sub == k, 0.0, cols[k] * inverse)
                top = top - ratio * row
                part = below[k] * inverse
                for m, head in enumerate(heads, k + 1):
                    cols[m] = cols[m] - ratio * head
                    if more:
                        below[m] = below[m] - part * head
                if more:
                    for j in range(SUB):
                        ahead[j] = ahead[j] - part * down(below[k], j)
            factor = jnp.where(lane < at + SUB, done, 0.0)
            out_ref[at : at + SUB, :] = factor
            near.append(jnp.where(lane < stop * SUB, factor, done))
            if not more:
                continue
            top = top * scale
            spread = [down(top, k) for k in range(SUB)]
            for t in range(b + 1, stop):
                kept = jnp.where(here, 0.0, rows[t])
                for k, column in enumerate(raw if t == b + 1 else across(rows[t], at)):
                    kept = kept - column * spread[k]
                rows[t] = kept
            cols = ahead
            if b + 2 < stop:
                below, ahead = across(rows[b + 2], at + SUB), across(rows[b + 2], at + 2 * SUB)
        if stop < count:
            pair = split(jnp.concatenate(near, axis=0))
            drop = product(pair, pair, ((0,), (0,)))
            for t in range(stop, count):
                rows[t] = jnp.where(lane < stop * SUB, 0.0, rows[t]) - drop[t * SUB : (t + 1) * SUB]


def pair_of(v):
    return jnp.concatenate(split(v), axis=1)


def weights(pair):
    hi, lo = pair[:, :LANES], pair[:, LANES:]
    return jnp.concatenate(
        [jnp.concatenate([hi, hi], axis=1), jnp.concatenate([lo, jnp.zeros_like(lo)], axis=1)], axis=0
    )


def folded(pair, weight):
    both = contract(pair, weight, NT)
    half = both.shape[1] // 2
    return both[:, :half] + both[:, half:]


def factor_panels(work_ref, pair_ref, weight_ref, inverse_ref):
    def panel(p, carry):
        mine = pl.ds(pl.multiple_of(p * LANES, LANES), LANES)

        def update(k, inner):
            work_ref[p] = work_ref[p] - folded(pair_ref[k], weights(pair_ref[k, mine, :]))
            return inner

        lax.fori_loop(0, p, update, 0)
        inverse_factor(work_ref[p, mine, :], inverse_ref)
        weight = weights(pair_of(inverse_ref[...]))
        solved = folded(pair_of(work_ref[p]), weight)
        weight_ref[p] = weight
        pair_ref[p] = pair_of(solved)
        work_ref[p] = solved
        return carry

    lax.fori_loop(0, work_ref.shape[0], panel, 0)


def packed_block(gram_ref, row, col, panels):
    at = sum(panels - p for p in range(col)) + row - col
    return gram_ref[at * LANES : (at + 1) * LANES, :]


def factor_kernel(scale, gram_ref, rows_ref, out_ref, work_ref, pair_ref, weight_ref, inverse_ref):
    panels = work_ref.shape[0]
    size = panels * LANES
    for p in range(panels):
        for r in range(panels):
            block = packed_block(gram_ref, r, p, panels) * scale if r >= p else jnp.zeros((LANES, LANES), F32)
            work_ref[p, r * LANES : (r + 1) * LANES, :] = block
        work_ref[p, size:, :] = rows_ref[:, p * LANES : (p + 1) * LANES]
    factor_panels(work_ref, pair_ref, weight_ref, inverse_ref)
    for p in range(panels):
        out_ref[:, p * LANES : (p + 1) * LANES] = work_ref[p, size:, :]


def factor_all(gram, rows, scale):
    count, width = rows.shape
    panels = width // LANES
    scratch = [
        pltpu.VMEM((panels, width + count, LANES), F32),
        pltpu.VMEM((panels, width + count, 2 * LANES), BF16),
        pltpu.VMEM((panels, 2 * LANES, 2 * LANES), BF16),
        pltpu.VMEM((LANES, LANES), F32),
    ]
    return kernel_call(lambda *refs: factor_kernel(scale, *refs), f32(count, width), scratch)(gram, rows)


def quarter_block(ref, second, at):
    part, at = divmod(at, ref.shape[2] // LANES)
    return ref[part, second, at * LANES : (at + 1) * LANES, :]


def triangle_block(ref, second, row, col, panels):
    return quarter_block(ref, second, sum(panels - p for p in range(col)) + row - col)


def first_kernel(scale, tri_ref, rows_ref, out_ref, pair_ref, weight_ref, work_ref, inverse_ref):
    panels = work_ref.shape[0]
    size = panels * LANES
    for p in range(panels):
        for r in range(panels):
            block = jnp.zeros((LANES, LANES), F32)
            if r >= p:
                block = triangle_block(tri_ref, 0, r, p, panels) * scale
            work_ref[p, r * LANES : (r + 1) * LANES, :] = block
        work_ref[p, size:, :] = rows_ref[:, p * LANES : (p + 1) * LANES]
    factor_panels(work_ref, pair_ref, weight_ref, inverse_ref)
    for p in range(panels):
        out_ref[:, p * LANES : (p + 1) * LANES] = work_ref[p, size:, :]


def second_kernel(
    scale, tri_ref, cross_ref, rows_ref, done_ref, pair_ref, weight_ref,
    out_ref, work_ref, left_ref, new_pair_ref, new_weight_ref, inverse_ref,
):
    panels = work_ref.shape[0]
    size = panels * LANES
    half = panels // 2
    for p in range(panels):
        blocks = []
        for r in range(panels):
            second, inner = divmod(r, half)
            blocks.append(quarter_block(cross_ref, second, p * half + inner))
        solve = jnp.concatenate(blocks, axis=0) * scale
        for k in range(p):
            pair = left_ref[:size, 2 * k * LANES : 2 * (k + 1) * LANES]
            solve = solve - folded(pair, weights(pair_ref[k, p * LANES : (p + 1) * LANES, :]))
        span = slice(2 * p * LANES, 2 * (p + 1) * LANES)
        left_ref[:size, span] = pair_of(folded(pair_of(solve), weight_ref[p]))
        left_ref[size:, span] = pair_ref[p, size:, :]
    for p in range(panels):
        mine = left_ref[p * LANES : (p + 1) * LANES, :]
        weight = jnp.concatenate(
            [weights(mine[:, 2 * k * LANES : 2 * (k + 1) * LANES]) for k in range(panels)], axis=1
        )
        drop = folded(left_ref[...], weight)
        for r in range(panels):
            block = jnp.zeros((LANES, LANES), F32)
            if r >= p:
                block = triangle_block(tri_ref, 1, r, p, panels) * scale - drop[r * LANES : (r + 1) * LANES]
            work_ref[p, r * LANES : (r + 1) * LANES, :] = block
        work_ref[p, size:, :] = rows_ref[:, size + p * LANES : size + (p + 1) * LANES] - drop[size:]
    factor_panels(work_ref, new_pair_ref, new_weight_ref, inverse_ref)
    out_ref[:, :size] = done_ref[...]
    for p in range(panels):
        out_ref[:, size + p * LANES : size + (p + 1) * LANES] = work_ref[p, size:, :]


def factor_halves(tri, cross, rows, scale):
    count, width = rows.shape
    size = width // 2
    panels = size // LANES
    total = size + count
    pairs, weight = (panels, total, 2 * LANES), (panels, 2 * LANES, 2 * LANES)
    work = [pltpu.VMEM((panels, total, LANES), F32)]
    inverse = [pltpu.VMEM((LANES, LANES), F32)]
    done, pair, mult = kernel_call(
        lambda *refs: first_kernel(scale, *refs),
        [f32(count, size), bf16(*pairs), bf16(*weight)],
        work + inverse,
    )(tri, rows)
    more = [pltpu.VMEM((total, panels * 2 * LANES), BF16), pltpu.VMEM(pairs, BF16), pltpu.VMEM(weight, BF16)]
    return kernel_call(
        lambda *refs: second_kernel(scale, *refs), f32(count, width), work + more + inverse
    )(tri, cross, rows, done, pair, mult)


def any_orb(part, top, scale):
    halo = top.shape[0]
    current = jnp.concatenate([part[:halo] + top, part[halo:]], axis=0)
    rows = lax.all_to_all(current, "orb", split_axis=0, concat_axis=1, tiled=True)
    panels = rows.shape[1] // LANES
    packed = LANES * panels * (panels + 1) // 2
    gram = kernel_call(gram_kernel, f32(packed, LANES))(rows)
    dom = bits("dom")
    return factor_all(summed(gram, dom[:1] + bits("orb") + dom[1:]), rows, scale)


def two_orb(part, top, scale):
    own, cols = part.shape
    halo = top.shape[0]
    second = lax.axis_index("orb")
    panels = cols // LANES
    packed = LANES * (panels * (panels + 1) // 2 + panels * (panels // 2))
    flag = second.reshape(1)
    low = exchanged(part[halo:], "orb", 1)
    gram = low_gram(flag, part, low, halo, packed)
    high = exchanged(part[:halo] + top, "orb", 1)
    gram = high_gram(flag, part, top, high, gram)
    dom = bits("dom")
    stages = dom if len(dom) < 4 else dom[:-2] + [("dom", dom[-2][1], 4)]
    gram = scattered(gram, stages)
    cut = LANES * panels * (panels + 1) // 2 // lax.axis_size("dom")
    tri, cross = [everywhere(piece, stages) for piece in (gram[:cut], gram[cut:])]
    mine = jnp.concatenate([part[:halo] + top, part[halo:]], axis=0).reshape(2, own // 2, cols)
    other = jnp.concatenate([high, low], axis=0).reshape(2, own // 2, cols)
    mine = jnp.where(second == 0, mine[0], mine[1])
    other = jnp.where(second == 0, other[0], other[1])
    rows = jnp.where(
        second == 0, jnp.concatenate([mine, other], axis=1), jnp.concatenate([other, mine], axis=1)
    )
    return factor_halves(tri, cross, rows, scale)


def everywhere(block, stages):
    for stage in reversed(stages[1:]):
        block = gathered(block, stage).reshape(-1, LANES)
    return gathered(gathered(block, ("orb", 1, 2)), stages[0])


def with_flag(body, out_shape, count, scratch=()):
    specs = [pl.BlockSpec(memory_space=pltpu.SMEM)] + [pl.BlockSpec(memory_space=pltpu.VMEM)] * count
    return pl.pallas_call(
        body,
        out_shape=out_shape,
        in_specs=specs,
        scratch_shapes=list(scratch),
        compiler_params=pltpu.CompilerParams(vmem_limit_bytes=VMEM_BYTES),
    )


def low_gram(flag, part, low, halo, packed):
    kernel = lambda *refs: low_gram_kernel(halo, *refs)
    return with_flag(kernel, f32(packed, LANES), 2)(flag, part, low)


def high_gram(flag, part, top, high, gram):
    kernel = lambda *refs: high_gram_kernel(lax.axis_size("dom"), *refs)
    return with_flag(kernel, f32(*gram.shape), 4, [pltpu.VMEM(gram.shape, F32)])(flag, part, top, high, gram)


def body(orbitals, cell_mats, cell_map):
    own, cols = orbitals.shape
    size = cell_mats.shape[1]
    node_total = own * lax.axis_size("dom")
    matrix = kernel_call(order_kernel, [bf16(size, size)] * 2)(cell_map, cell_mats)
    part, top = filtered_columns(orbitals, matrix)
    panels = cols // LANES
    two = (
        lax.axis_size("orb") == 2
        and lax.axis_size("dom") > 1
        and cols % (2 * LANES) == 0
        and (LANES * panels * (panels + 1) // 2) % lax.axis_size("dom") == 0
        and (LANES * panels * panels // 2) % lax.axis_size("dom") == 0
    )
    return (two_orb if two else any_orb)(part, top, 1.0 / node_total)


def solution(mesh):
    placed = (P("dom", "orb"), P("dom", None, None), P("dom", None))
    return jax.shard_map(
        body, mesh=mesh, in_specs=placed, out_specs=P(("dom", "orb"), None), check_vma=False
    )
```

```python
import jax
import jax.numpy as jnp
from jax import lax
from jax.experimental import pallas as pl
from jax.experimental.pallas import tpu as pltpu
from jax.sharding import PartitionSpec as P

DEGREE = 5

filter_center = 2.0
filter_half = 3.5

F32, BF16 = jnp.float32, jnp.bfloat16
LANES, SUB = 128, 8
VMEM_BYTES = 24 << 20


def kernel_call(body, out_shape, scratch=()):
    return pl.pallas_call(
        body,
        out_shape=out_shape,
        scratch_shapes=list(scratch),
        compiler_params=pltpu.CompilerParams(vmem_limit_bytes=VMEM_BYTES),
    )


def f32(*shape):
    return jax.ShapeDtypeStruct(shape, F32)


def bf16(*shape):
    return jax.ShapeDtypeStruct(shape, BF16)


def split(v):
    hi = v.astype(BF16)
    return hi, (v - hi.astype(F32)).astype(BF16)


def contract(a, b, dims):
    return lax.dot_general(a, b, (dims, ((), ())), preferred_element_type=F32)


def product(a, b, dims):
    (a_hi, a_lo), (b_hi, b_lo) = a, b
    return contract(a_hi, b_hi, dims) + (contract(a_hi, b_lo, dims) + contract(a_lo, b_hi, dims))


NN = ((1,), (0,))
NT = ((1,), (1,))


def order_kernel(map_ref, cell_ref, hi_ref, lo_ref):
    size = cell_ref.shape[1]
    node = lax.broadcasted_iota(jnp.int32, (size, size), 0)
    pick = jnp.where(node == map_ref[...], 1.0, 0.0).astype(BF16)
    for half, out_ref in zip(split(cell_ref[0]), (hi_ref, lo_ref)):
        rows = contract(pick, half, NN).astype(BF16)
        out_ref[...] = contract(rows, pick, NT).astype(BF16)


def first_kernel_of_filter(hi_ref, lo_ref, own_ref, applied_ref):
    own = own_ref.shape[0]
    scale = 1.0 / filter_half
    applied_ref[...] = product((hi_ref[:, :own], lo_ref[:, :own]), split(own_ref[...]), NN) * scale


def edge_columns(ref, own, first, rows=slice(None)):
    right = ref[rows, own:]
    if first:
        return right
    return jnp.concatenate([ref[rows, : ref.shape[1] - own], right], axis=1)


def edge_kernel(order, own, hi_ref, lo_ref, applied_ref, *refs):
    halo = hi_ref.shape[0] - own
    scale = (1.0 if order == 0 else 2.0) / filter_half
    count = 1 if order == 0 else 2
    delta = split(jnp.concatenate([ref[...] for ref in refs[:count]], axis=0))
    outs = refs[count:]
    spans = [slice(own, own + halo)] if order == DEGREE - 1 else [slice(0, halo), slice(own, own + halo)]
    for span, out_ref in zip(spans, outs):
        block = [edge_columns(ref, own, order == 0, span) for ref in (hi_ref, lo_ref)]
        out_ref[...] = applied_ref[span, :] + product(block, delta, NN) * scale


def rest_kernel(order, own, hi_ref, lo_ref, applied_ref, vec_ref, *refs):
    halo = hi_ref.shape[0] - own
    scale = (1.0 if order == 0 else 2.0) / filter_half
    last = order == DEGREE - 1
    if order == 0:
        bottom = refs[0][...]
        delta, outs = bottom, refs[1:]
        vec = jnp.concatenate([vec_ref[...], bottom], axis=0)
    else:
        top, bottom, before_ref = refs[0][...], refs[1][...], refs[2]
        delta, outs = jnp.concatenate([top, bottom], axis=0), refs[3:]
        vec = jnp.concatenate(
            [vec_ref[:halo, :] + top, vec_ref[halo:own, :], vec_ref[own:, :] + bottom], axis=0
        )
    rows = slice(0, own) if last else slice(0, own + halo)
    columns = [edge_columns(ref, own, order == 0, rows) for ref in (hi_ref, lo_ref)]
    part = applied_ref[rows, :] + product(columns, split(delta), NN) * scale
    part = part - (filter_center * scale) * vec[rows]
    if order > 0:
        part = part - before_ref[rows, :]
    outs[0][...] = part
    if not last:
        outs[1][...] = vec
        outs[2][...] = product((hi_ref[...], lo_ref[...]), split(part), NN) * (2.0 / filter_half)


def shifted(block, axis, distance):
    count = lax.axis_size(axis)
    route = [((i - distance) % count, i) for i in range(count)]
    return lax.ppermute(block, axis, route)


def filtered_columns(orbitals, matrix):
    own, cols = orbitals.shape
    size = matrix[0].shape[0]
    halo = size - own
    arrived = (shifted(orbitals[:halo], "dom", -1),)
    applied = kernel_call(first_kernel_of_filter, f32(size, cols))(*matrix, orbitals)
    vec, before = orbitals, ()
    for order in range(DEGREE):
        last = order == DEGREE - 1
        edge = lambda *refs, order=order: edge_kernel(order, own, *refs)
        rest = lambda *refs, order=order: rest_kernel(order, own, *refs)
        sent = kernel_call(edge, [f32(halo, cols)] * (1 if last else 2))(*matrix, applied, *arrived)
        moved = [shifted(sent[-1], "dom", 1)]
        if not last:
            moved.append(shifted(sent[0], "dom", -1))
        outs = [f32(own, cols)] if last else [f32(size, cols)] * 3
        got = kernel_call(rest, outs)(*matrix, applied, vec, *arrived, *before)
        if last:
            return got[0], moved[0]
        vec, before, applied = got[0], (got[1],), got[2]
        arrived = tuple(moved)


def gram_kernel(rows_ref, out_ref):
    hi, lo = split(rows_ref[...].T)
    panels = hi.shape[0] // LANES
    at = 0
    for p in range(panels):
        cut = slice(p * LANES, (p + 1) * LANES)
        below = hi.shape[0] - p * LANES
        out_ref[at : at + below, :] = product((hi[p * LANES :], lo[p * LANES :]), (hi[cut], lo[cut]), NT)
        at += below


def half_gram(mine, other, second, out_ref, base_ref):
    own, own_lo = split(mine.T)
    other, other_lo = split(other.T)
    cols = own.shape[0]
    half = cols // 2

    def put(at, value):
        span = slice(at, at + value.shape[0])
        out_ref[span, :] = value if base_ref is None else base_ref[span, :] + value

    at = 0
    for p in range(0, cols, LANES):
        put(at, product((own[p:], own_lo[p:]), (own[p : p + LANES], own_lo[p : p + LANES]), NT))
        at += cols - p

    def cross(left, right):
        for i, p in enumerate(range(0, cols, LANES)):
            cut = slice(p, p + LANES)
            put(at + i * half, product(left, (right[0][cut], right[1][cut]), NT))

    @pl.when(second == 0)
    def _():
        cross((other[:half], other_lo[:half]), (own, own_lo))

    @pl.when(second == 1)
    def _():
        cross((own[half:], own_lo[half:]), (other, other_lo))


def low_gram_kernel(halo, second_ref, mine_ref, other_ref, out_ref):
    half_gram(mine_ref[halo:, :], other_ref[...], second_ref[0], out_ref, None)


def high_gram_kernel(pieces, flag_ref, part_ref, top_ref, other_ref, base_ref, keep_ref, send_ref, all_ref):
    halo = top_ref.shape[0]
    half_gram(part_ref[:halo, :] + top_ref[...], other_ref[...], flag_ref[1], all_ref, base_ref)
    panels = top_ref.shape[1] // LANES
    total = all_ref.shape[0]
    cut = LANES * panels * (panels + 1) // 2
    a, b, piece = cut // pieces, (total - cut) // pieces, total // pieces

    def put(out_ref, first):
        for at in range(pieces // 2):
            i = first + at
            out_ref[at * piece : at * piece + a, :] = all_ref[i * a : (i + 1) * a, :]
            out_ref[at * piece + a : (at + 1) * piece, :] = all_ref[cut + i * b : cut + (i + 1) * b, :]

    @pl.when(flag_ref[0] == 0)
    def _():
        put(keep_ref, 0)
        put(send_ref, pieces // 2)

    @pl.when(flag_ref[0] == 1)
    def _():
        put(keep_ref, pieces // 2)
        put(send_ref, 0)


def exchanged(block, axis, mask):
    route = [(i, i ^ mask) for i in range(lax.axis_size(axis))]
    return lax.ppermute(block, axis, route)


def bits(axis):
    count = lax.axis_size(axis)
    return [(axis, 1 << i, 2) for i in range(count.bit_length() - 1)]


def rank(axis, unit, count):
    return (lax.axis_index(axis) // unit) % count


def scattered(block, stages):
    for axis, unit, count in stages:
        mine = rank(axis, unit, count)
        pieces = block.reshape(count, -1, block.shape[-1])
        total = lax.dynamic_index_in_dim(pieces, mine, keepdims=False)
        for d in range(1, count):
            piece = lax.dynamic_index_in_dim(pieces, mine ^ d, keepdims=False)
            total = total + exchanged(piece, axis, d * unit)
        block = total
    return block


def gathered(block, stage):
    axis, unit, count = stage
    mine = rank(axis, unit, count)
    pieces = jnp.stack([block] + [exchanged(block, axis, d * unit) for d in range(1, count)])
    bit = 1
    while bit < count:
        pair = pieces.reshape((count // (2 * bit), 2, bit) + block.shape)
        pieces = jnp.where((mine & bit) != 0, pair[:, ::-1], pair).reshape(pieces.shape)
        bit *= 2
    return pieces


def summed(block, stages):
    width = block.shape[-1]
    block = scattered(block, stages)
    for stage in reversed(stages):
        block = gathered(block, stage).reshape(-1, width)
    return block


def inverse_factor(block, out_ref):
    size = block.shape[0]
    count = size // SUB
    shape = (SUB, size)
    rows = [block[t : t + SUB] for t in range(0, size, SUB)]
    sub = lax.broadcasted_iota(jnp.int32, shape, 0)
    lane = lax.broadcasted_iota(jnp.int32, shape, 1)

    def across(v, at):
        return [jnp.broadcast_to(v[:, at + k : at + k + 1], shape) for k in range(SUB)]

    def down(v, k):
        return jnp.broadcast_to(v[k : k + 1], shape)

    for start in range(0, count, count // 2):
        stop, at = start + count // 2, start * SUB
        cols, below = across(rows[start], at), across(rows[start + 1], at)
        ahead = across(rows[start + 1], at + SUB)
        near = []
        for b in range(start, stop):
            at = b * SUB
            more = b + 1 < stop
            raw = list(below)
            here = (lane >= at) & (lane < at + SUB)
            top = jnp.where(here, jnp.where(lane - at == sub, 1.0, 0.0), rows[b])
            scale = jnp.zeros(shape, F32)
            done = jnp.zeros(shape, F32)
            pivot = down(cols[0], 0)
            for k in range(SUB):
                inverse = 1.0 / pivot
                row = down(top, k)
                done = jnp.where(sub == k, row * lax.rsqrt(pivot), done)
                scale = jnp.where(sub == k, inverse, scale)
                heads = [down(cols[m], k) for m in range(k + 1, SUB)]
                if heads:
                    pivot = down(cols[k + 1], k + 1) - (heads[0] * inverse) * heads[0]
                ratio = jnp.where(sub == k, 0.0, cols[k] * inverse)
                top = top - ratio * row
                part = below[k] * inverse
                for m, head in enumerate(heads, k + 1):
                    cols[m] = cols[m] - ratio * head
                    if more:
                        below[m] = below[m] - part * head
                if more:
                    for j in range(SUB):
                        ahead[j] = ahead[j] - part * down(below[k], j)
            factor = jnp.where(lane < at + SUB, done, 0.0)
            out_ref[at : at + SUB, :] = factor
            near.append(jnp.where(lane < stop * SUB, factor, done))
            if not more:
                continue
            top = top * scale
            spread = [down(top, k) for k in range(SUB)]
            for t in range(b + 1, stop):
                kept = jnp.where(here, 0.0, rows[t])
                for k, column in enumerate(raw if t == b + 1 else across(rows[t], at)):
                    kept = kept - column * spread[k]
                rows[t] = kept
            cols = ahead
            if b + 2 < stop:
                below, ahead = across(rows[b + 2], at + SUB), across(rows[b + 2], at + 2 * SUB)
        if stop < count:
            pair = split(jnp.concatenate(near, axis=0))
            drop = product(pair, pair, ((0,), (0,)))
            for t in range(stop, count):
                rows[t] = jnp.where(lane < stop * SUB, 0.0, rows[t]) - drop[t * SUB : (t + 1) * SUB]


def pair_of(v):
    return jnp.concatenate(split(v), axis=1)


def weights(pair):
    hi, lo = pair[:, :LANES], pair[:, LANES:]
    return jnp.concatenate(
        [jnp.concatenate([hi, hi], axis=1), jnp.concatenate([lo, jnp.zeros_like(lo)], axis=1)], axis=0
    )


def folded(pair, weight):
    both = contract(pair, weight, NT)
    half = both.shape[1] // 2
    return both[:, :half] + both[:, half:]


def factor_panels(work_ref, pair_ref, weight_ref, inverse_ref):
    def panel(p, carry):
        mine = pl.ds(pl.multiple_of(p * LANES, LANES), LANES)

        def update(k, inner):
            work_ref[p] = work_ref[p] - folded(pair_ref[k], weights(pair_ref[k, mine, :]))
            return inner

        lax.fori_loop(0, p, update, 0)
        inverse_factor(work_ref[p, mine, :], inverse_ref)
        weight = weights(pair_of(inverse_ref[...]))
        solved = folded(pair_of(work_ref[p]), weight)
        weight_ref[p] = weight
        pair_ref[p] = pair_of(solved)
        work_ref[p] = solved
        return carry

    lax.fori_loop(0, work_ref.shape[0], panel, 0)


def packed_block(gram_ref, row, col, panels):
    at = sum(panels - p for p in range(col)) + row - col
    return gram_ref[at * LANES : (at + 1) * LANES, :]


def factor_kernel(scale, gram_ref, rows_ref, out_ref, work_ref, pair_ref, weight_ref, inverse_ref):
    panels = work_ref.shape[0]
    size = panels * LANES
    for p in range(panels):
        for r in range(panels):
            block = packed_block(gram_ref, r, p, panels) * scale if r >= p else jnp.zeros((LANES, LANES), F32)
            work_ref[p, r * LANES : (r + 1) * LANES, :] = block
        work_ref[p, size:, :] = rows_ref[:, p * LANES : (p + 1) * LANES]
    factor_panels(work_ref, pair_ref, weight_ref, inverse_ref)
    for p in range(panels):
        out_ref[:, p * LANES : (p + 1) * LANES] = work_ref[p, size:, :]


def factor_all(gram, rows, scale):
    count, width = rows.shape
    panels = width // LANES
    scratch = [
        pltpu.VMEM((panels, width + count, LANES), F32),
        pltpu.VMEM((panels, width + count, 2 * LANES), BF16),
        pltpu.VMEM((panels, 2 * LANES, 2 * LANES), BF16),
        pltpu.VMEM((LANES, LANES), F32),
    ]
    return kernel_call(lambda *refs: factor_kernel(scale, *refs), f32(count, width), scratch)(gram, rows)


def quarter_block(ref, second, at):
    part, at = divmod(at, ref.shape[2] // LANES)
    return ref[part, second, at * LANES : (at + 1) * LANES, :]


def cross_block(ref, second, at):
    rows = ref.shape[3] // LANES
    part, at = divmod(at, ref.shape[1] * rows)
    piece, at = divmod(at, rows)
    return ref[part, piece, second, at * LANES : (at + 1) * LANES, :]


def triangle_block(ref, second, row, col, panels):
    return quarter_block(ref, second, sum(panels - p for p in range(col)) + row - col)


def first_kernel(scale, tri_ref, rows_ref, out_ref, pair_ref, weight_ref, work_ref, inverse_ref):
    panels = work_ref.shape[0]
    size = panels * LANES
    for p in range(panels):
        for r in range(panels):
            block = jnp.zeros((LANES, LANES), F32)
            if r >= p:
                block = triangle_block(tri_ref, 0, r, p, panels) * scale
            work_ref[p, r * LANES : (r + 1) * LANES, :] = block
        work_ref[p, size:, :] = rows_ref[:, p * LANES : (p + 1) * LANES]
    factor_panels(work_ref, pair_ref, weight_ref, inverse_ref)
    for p in range(panels):
        out_ref[:, p * LANES : (p + 1) * LANES] = work_ref[p, size:, :]


def second_kernel(
    scale, tri_ref, cross_ref, rows_ref, done_ref, pair_ref, weight_ref,
    out_ref, work_ref, left_ref, new_pair_ref, new_weight_ref, inverse_ref,
):
    panels = work_ref.shape[0]
    size = panels * LANES
    half = panels // 2
    for p in range(panels):
        blocks = []
        for r in range(panels):
            second, inner = divmod(r, half)
            blocks.append(cross_block(cross_ref, second, p * half + inner))
        solve = jnp.concatenate(blocks, axis=0) * scale
        for k in range(p):
            pair = left_ref[:size, 2 * k * LANES : 2 * (k + 1) * LANES]
            solve = solve - folded(pair, weights(pair_ref[k, p * LANES : (p + 1) * LANES, :]))
        span = slice(2 * p * LANES, 2 * (p + 1) * LANES)
        left_ref[:size, span] = pair_of(folded(pair_of(solve), weight_ref[p]))
        left_ref[size:, span] = pair_ref[p, size:, :]
    for p in range(panels):
        mine = left_ref[p * LANES : (p + 1) * LANES, :]
        weight = jnp.concatenate(
            [weights(mine[:, 2 * k * LANES : 2 * (k + 1) * LANES]) for k in range(panels)], axis=1
        )
        drop = folded(left_ref[p * LANES :, :], weight)
        for r in range(panels):
            block = jnp.zeros((LANES, LANES), F32)
            if r >= p:
                block = triangle_block(tri_ref, 1, r, p, panels) * scale - drop[(r - p) * LANES : (r - p + 1) * LANES]
            work_ref[p, r * LANES : (r + 1) * LANES, :] = block
        work_ref[p, size:, :] = rows_ref[:, size + p * LANES : size + (p + 1) * LANES] - drop[size - p * LANES :]
    factor_panels(work_ref, new_pair_ref, new_weight_ref, inverse_ref)
    out_ref[:, :size] = done_ref[...]
    for p in range(panels):
        out_ref[:, size + p * LANES : size + (p + 1) * LANES] = work_ref[p, size:, :]


def factor_halves(tri, cross, rows, scale):
    count, width = rows.shape
    size = width // 2
    panels = size // LANES
    total = size + count
    pairs, weight = (panels, total, 2 * LANES), (panels, 2 * LANES, 2 * LANES)
    work = [pltpu.VMEM((panels, total, LANES), F32)]
    inverse = [pltpu.VMEM((LANES, LANES), F32)]
    done, pair, mult = kernel_call(
        lambda *refs: first_kernel(scale, *refs),
        [f32(count, size), bf16(*pairs), bf16(*weight)],
        work + inverse,
    )(tri, rows)
    more = [pltpu.VMEM((total, panels * 2 * LANES), BF16), pltpu.VMEM(pairs, BF16), pltpu.VMEM(weight, BF16)]
    return kernel_call(
        lambda *refs: second_kernel(scale, *refs), f32(count, width), work + more + inverse
    )(tri, cross, rows, done, pair, mult)


def any_orb(part, top, scale):
    halo = top.shape[0]
    current = jnp.concatenate([part[:halo] + top, part[halo:]], axis=0)
    rows = lax.all_to_all(current, "orb", split_axis=0, concat_axis=1, tiled=True)
    panels = rows.shape[1] // LANES
    packed = LANES * panels * (panels + 1) // 2
    gram = kernel_call(gram_kernel, f32(packed, LANES))(rows)
    dom = bits("dom")
    return factor_all(summed(gram, dom[:1] + bits("orb") + dom[1:]), rows, scale)


def two_orb(part, top, scale):
    own, cols = part.shape
    halo = top.shape[0]
    second = lax.axis_index("orb")
    panels = cols // LANES
    packed = LANES * (panels * (panels + 1) // 2 + panels * (panels // 2))
    flag = second.reshape(1)
    low = exchanged(part[halo:], "orb", 1)
    gram = low_gram(flag, part, low, halo, packed)
    high = exchanged(part[:halo] + top, "orb", 1)
    dom = bits("dom")
    stages = dom if len(dom) < 4 else dom[:-2] + [("dom", dom[-2][1], 4)]
    flags = jnp.stack([rank(*stages[0]), second])
    keep, send = high_gram(flags, part, top, high, gram)
    gram = scattered(keep + exchanged(send, "dom", stages[0][1]), stages[1:])
    cut = LANES * panels * (panels + 1) // 2 // lax.axis_size("dom")
    orb = ("orb", 1, 2)
    tri = everywhere(gram[:cut], stages[:0:-1] + [orb, stages[0]])
    cross = everywhere(gram[cut:], stages[:1:-1] + [orb, stages[1], stages[0]])
    tri = tri.reshape(2, 2, -1, LANES)
    cross = cross.reshape(2, stages[1][2], 2, -1, LANES)
    mine = jnp.concatenate([part[:halo] + top, part[halo:]], axis=0).reshape(2, own // 2, cols)
    other = jnp.concatenate([high, low], axis=0).reshape(2, own // 2, cols)
    mine = jnp.where(second == 0, mine[0], mine[1])
    other = jnp.where(second == 0, other[0], other[1])
    rows = jnp.where(
        second == 0, jnp.concatenate([mine, other], axis=1), jnp.concatenate([other, mine], axis=1)
    )
    return factor_halves(tri, cross, rows, scale)


def everywhere(block, stages):
    for stage in stages:
        block = gathered(block, stage).reshape(-1, LANES)
    return block


def with_flag(body, out_shape, count, scratch=()):
    specs = [pl.BlockSpec(memory_space=pltpu.SMEM)] + [pl.BlockSpec(memory_space=pltpu.VMEM)] * count
    return pl.pallas_call(
        body,
        out_shape=out_shape,
        in_specs=specs,
        scratch_shapes=list(scratch),
        compiler_params=pltpu.CompilerParams(vmem_limit_bytes=VMEM_BYTES),
    )


def low_gram(flag, part, low, halo, packed):
    kernel = lambda *refs: low_gram_kernel(halo, *refs)
    return with_flag(kernel, f32(packed, LANES), 2)(flag, part, low)


def high_gram(flags, part, top, high, gram):
    kernel = lambda *refs: high_gram_kernel(lax.axis_size("dom"), *refs)
    outs = [f32(gram.shape[0] // 2, LANES)] * 2
    return with_flag(kernel, outs, 4, [pltpu.VMEM(gram.shape, F32)])(flags, part, top, high, gram)


def body(orbitals, cell_mats, cell_map):
    own, cols = orbitals.shape
    size = cell_mats.shape[1]
    node_total = own * lax.axis_size("dom")
    matrix = kernel_call(order_kernel, [bf16(size, size)] * 2)(cell_map, cell_mats)
    part, top = filtered_columns(orbitals, matrix)
    panels = cols // LANES
    two = (
        lax.axis_size("orb") == 2
        and lax.axis_size("dom") > 2
        and cols % (2 * LANES) == 0
        and (LANES * panels * (panels + 1) // 2) % lax.axis_size("dom") == 0
        and panels * panels // 2 % 4 == 0
        and (LANES * panels * panels // 2) % lax.axis_size("dom") == 0
    )
    return (two_orb if two else any_orb)(part, top, 1.0 / node_total)


def solution(mesh):
    placed = (P("dom", "orb"), P("dom", None, None), P("dom", None))
    return jax.shard_map(
        body, mesh=mesh, in_specs=placed, out_specs=P(("dom", "orb"), None), check_vma=False
    )
```

```python
import jax
import jax.numpy as jnp
from jax import lax
from jax.experimental import pallas as pl
from jax.experimental.pallas import tpu as pltpu
from jax.sharding import PartitionSpec as P

DEGREE = 5

filter_center = 2.0
filter_half = 3.5

F32, BF16 = jnp.float32, jnp.bfloat16
LANES, SUB = 128, 8
VMEM_BYTES = 24 << 20


def kernel_call(body, out_shape, scratch=()):
    return pl.pallas_call(
        body,
        out_shape=out_shape,
        scratch_shapes=list(scratch),
        compiler_params=pltpu.CompilerParams(vmem_limit_bytes=VMEM_BYTES),
    )


def f32(*shape):
    return jax.ShapeDtypeStruct(shape, F32)


def bf16(*shape):
    return jax.ShapeDtypeStruct(shape, BF16)


def split(v):
    hi = v.astype(BF16)
    return hi, (v - hi.astype(F32)).astype(BF16)


def contract(a, b, dims):
    return lax.dot_general(a, b, (dims, ((), ())), preferred_element_type=F32)


def product(a, b, dims):
    (a_hi, a_lo), (b_hi, b_lo) = a, b
    return contract(a_hi, b_hi, dims) + (contract(a_hi, b_lo, dims) + contract(a_lo, b_hi, dims))


NN = ((1,), (0,))
NT = ((1,), (1,))


def order_kernel(map_ref, cell_ref, hi_ref, lo_ref):
    size = cell_ref.shape[1]
    node = lax.broadcasted_iota(jnp.int32, (size, size), 0)
    pick = jnp.where(node == map_ref[...], 1.0, 0.0).astype(BF16)
    for half, out_ref in zip(split(cell_ref[0]), (hi_ref, lo_ref)):
        rows = contract(pick, half, NN).astype(BF16)
        out_ref[...] = contract(rows, pick, NT).astype(BF16)


def first_kernel_of_filter(hi_ref, lo_ref, own_ref, applied_ref):
    own = own_ref.shape[0]
    scale = 1.0 / filter_half
    applied_ref[...] = product((hi_ref[:, :own], lo_ref[:, :own]), split(own_ref[...]), NN) * scale


def edge_columns(ref, own, first, rows=slice(None)):
    right = ref[rows, own:]
    if first:
        return right
    return jnp.concatenate([ref[rows, : ref.shape[1] - own], right], axis=1)


def edge_kernel(order, own, hi_ref, lo_ref, applied_ref, *refs):
    halo = hi_ref.shape[0] - own
    scale = (1.0 if order == 0 else 2.0) / filter_half
    count = 1 if order == 0 else 2
    delta = split(jnp.concatenate([ref[...] for ref in refs[:count]], axis=0))
    outs = refs[count:]
    spans = [slice(own, own + halo)] if order == DEGREE - 1 else [slice(0, halo), slice(own, own + halo)]
    for span, out_ref in zip(spans, outs):
        block = [edge_columns(ref, own, order == 0, span) for ref in (hi_ref, lo_ref)]
        out_ref[...] = applied_ref[span, :] + product(block, delta, NN) * scale


def rest_kernel(order, own, hi_ref, lo_ref, applied_ref, vec_ref, *refs):
    halo = hi_ref.shape[0] - own
    scale = (1.0 if order == 0 else 2.0) / filter_half
    last = order == DEGREE - 1
    if order == 0:
        bottom = refs[0][...]
        delta, outs = bottom, refs[1:]
        vec = jnp.concatenate([vec_ref[...], bottom], axis=0)
    else:
        top, bottom, before_ref = refs[0][...], refs[1][...], refs[2]
        delta, outs = jnp.concatenate([top, bottom], axis=0), refs[3:]
        vec = jnp.concatenate(
            [vec_ref[:halo, :] + top, vec_ref[halo:own, :], vec_ref[own:, :] + bottom], axis=0
        )
    rows = slice(0, own) if last else slice(0, own + halo)
    columns = [edge_columns(ref, own, order == 0, rows) for ref in (hi_ref, lo_ref)]
    part = applied_ref[rows, :] + product(columns, split(delta), NN) * scale
    part = part - (filter_center * scale) * vec[rows]
    if order > 0:
        part = part - before_ref[rows, :]
    outs[0][...] = part
    if not last:
        outs[1][...] = vec
        outs[2][...] = product((hi_ref[...], lo_ref[...]), split(part), NN) * (2.0 / filter_half)


def shifted(block, axis, distance):
    count = lax.axis_size(axis)
    route = [((i - distance) % count, i) for i in range(count)]
    return lax.ppermute(block, axis, route)


def filtered_columns(orbitals, matrix):
    own, cols = orbitals.shape
    size = matrix[0].shape[0]
    halo = size - own
    arrived = (shifted(orbitals[:halo], "dom", -1),)
    applied = kernel_call(first_kernel_of_filter, f32(size, cols))(*matrix, orbitals)
    vec, before = orbitals, ()
    for order in range(DEGREE):
        last = order == DEGREE - 1
        edge = lambda *refs, order=order: edge_kernel(order, own, *refs)
        rest = lambda *refs, order=order: rest_kernel(order, own, *refs)
        sent = kernel_call(edge, [f32(halo, cols)] * (1 if last else 2))(*matrix, applied, *arrived)
        moved = [shifted(sent[-1], "dom", 1)]
        if not last:
            moved.append(shifted(sent[0], "dom", -1))
        outs = [f32(own, cols)] if last else [f32(size, cols)] * 3
        got = kernel_call(rest, outs)(*matrix, applied, vec, *arrived, *before)
        if last:
            return got[0], moved[0]
        vec, before, applied = got[0], (got[1],), got[2]
        arrived = tuple(moved)


def gram_kernel(rows_ref, out_ref):
    hi, lo = split(rows_ref[...].T)
    panels = hi.shape[0] // LANES
    at = 0
    for p in range(panels):
        cut = slice(p * LANES, (p + 1) * LANES)
        below = hi.shape[0] - p * LANES
        out_ref[at : at + below, :] = product((hi[p * LANES :], lo[p * LANES :]), (hi[cut], lo[cut]), NT)
        at += below


def half_gram(mine, other, second, out_ref, base_ref):
    own, own_lo = split(mine.T)
    other, other_lo = split(other.T)
    cols = own.shape[0]
    half = cols // 2

    def put(at, value):
        span = slice(at, at + value.shape[0])
        out_ref[span, :] = value if base_ref is None else base_ref[span, :] + value

    at = 0
    for p in range(0, cols, LANES):
        put(at, product((own[p:], own_lo[p:]), (own[p : p + LANES], own_lo[p : p + LANES]), NT))
        at += cols - p

    def cross(left, right):
        for i, p in enumerate(range(0, cols, LANES)):
            cut = slice(p, p + LANES)
            put(at + i * half, product(left, (right[0][cut], right[1][cut]), NT))

    @pl.when(second == 0)
    def _():
        cross((other[:half], other_lo[:half]), (own, own_lo))

    @pl.when(second == 1)
    def _():
        cross((own[half:], own_lo[half:]), (other, other_lo))


def low_gram_kernel(halo, second_ref, mine_ref, other_ref, out_ref):
    half_gram(mine_ref[halo:, :], other_ref[...], second_ref[0], out_ref, None)


def high_gram_kernel(pieces, flag_ref, part_ref, top_ref, other_ref, base_ref, keep_ref, send_ref, all_ref):
    halo = top_ref.shape[0]
    half_gram(part_ref[:halo, :] + top_ref[...], other_ref[...], flag_ref[1], all_ref, base_ref)
    panels = top_ref.shape[1] // LANES
    total = all_ref.shape[0]
    cut = LANES * panels * (panels + 1) // 2
    a, b, piece = cut // pieces, (total - cut) // pieces, total // pieces

    def put(out_ref, first):
        for at in range(pieces // 2):
            i = first + at
            out_ref[at * piece : at * piece + a, :] = all_ref[i * a : (i + 1) * a, :]
            out_ref[at * piece + a : (at + 1) * piece, :] = all_ref[cut + i * b : cut + (i + 1) * b, :]

    @pl.when(flag_ref[0] == 0)
    def _():
        put(keep_ref, 0)
        put(send_ref, pieces // 2)

    @pl.when(flag_ref[0] == 1)
    def _():
        put(keep_ref, pieces // 2)
        put(send_ref, 0)


def exchanged(block, axis, mask):
    route = [(i, i ^ mask) for i in range(lax.axis_size(axis))]
    return lax.ppermute(block, axis, route)


def bits(axis):
    count = lax.axis_size(axis)
    return [(axis, 1 << i, 2) for i in range(count.bit_length() - 1)]


def rank(axis, unit, count):
    return (lax.axis_index(axis) // unit) % count


def scattered(block, stages):
    for axis, unit, count in stages:
        mine = rank(axis, unit, count)
        pieces = block.reshape(count, -1, block.shape[-1])
        total = lax.dynamic_index_in_dim(pieces, mine, keepdims=False)
        for d in range(1, count):
            piece = lax.dynamic_index_in_dim(pieces, mine ^ d, keepdims=False)
            total = total + exchanged(piece, axis, d * unit)
        block = total
    return block


def gathered(block, stage):
    axis, unit, count = stage
    mine = rank(axis, unit, count)
    pieces = jnp.stack([block] + [exchanged(block, axis, d * unit) for d in range(1, count)])
    bit = 1
    while bit < count:
        pair = pieces.reshape((count // (2 * bit), 2, bit) + block.shape)
        pieces = jnp.where((mine & bit) != 0, pair[:, ::-1], pair).reshape(pieces.shape)
        bit *= 2
    return pieces


def summed(block, stages):
    width = block.shape[-1]
    block = scattered(block, stages)
    for stage in reversed(stages):
        block = gathered(block, stage).reshape(-1, width)
    return block


def inverse_factor(block, out_ref):
    size = block.shape[0]
    count = size // SUB
    shape = (SUB, size)
    rows = [block[t : t + SUB] for t in range(0, size, SUB)]
    sub = lax.broadcasted_iota(jnp.int32, shape, 0)
    lane = lax.broadcasted_iota(jnp.int32, shape, 1)

    def across(v, at):
        return [jnp.broadcast_to(v[:, at + k : at + k + 1], shape) for k in range(SUB)]

    def down(v, k):
        return jnp.broadcast_to(v[k : k + 1], shape)

    for start in range(0, count, count // 2):
        stop, at = start + count // 2, start * SUB
        cols, below = across(rows[start], at), across(rows[start + 1], at)
        ahead = across(rows[start + 1], at + SUB)
        near = []
        for b in range(start, stop):
            at = b * SUB
            more = b + 1 < stop
            raw = list(below)
            here = (lane >= at) & (lane < at + SUB)
            top = jnp.where(here, jnp.where(lane - at == sub, 1.0, 0.0), rows[b])
            scale = jnp.zeros(shape, F32)
            done = jnp.zeros(shape, F32)
            pivot = down(cols[0], 0)
            for k in range(SUB):
                inverse = 1.0 / pivot
                row = down(top, k)
                done = jnp.where(sub == k, row * lax.rsqrt(pivot), done)
                scale = jnp.where(sub == k, inverse, scale)
                heads = [down(cols[m], k) for m in range(k + 1, SUB)]
                if heads:
                    pivot = down(cols[k + 1], k + 1) - (heads[0] * inverse) * heads[0]
                ratio = jnp.where(sub == k, 0.0, cols[k] * inverse)
                top = top - ratio * row
                part = below[k] * inverse
                for m, head in enumerate(heads, k + 1):
                    cols[m] = cols[m] - ratio * head
                    if more:
                        below[m] = below[m] - part * head
                if more:
                    for j in range(SUB):
                        ahead[j] = ahead[j] - part * down(below[k], j)
            factor = jnp.where(lane < at + SUB, done, 0.0)
            out_ref[at : at + SUB, :] = factor
            near.append(jnp.where(lane < stop * SUB, factor, done))
            if not more:
                continue
            top = top * scale
            spread = [down(top, k) for k in range(SUB)]
            for t in range(b + 1, stop):
                kept = jnp.where(here, 0.0, rows[t])
                for k, column in enumerate(raw if t == b + 1 else across(rows[t], at)):
                    kept = kept - column * spread[k]
                rows[t] = kept
            cols = ahead
            if b + 2 < stop:
                below, ahead = across(rows[b + 2], at + SUB), across(rows[b + 2], at + 2 * SUB)
        if stop < count:
            pair = split(jnp.concatenate(near, axis=0))
            drop = product(pair, pair, ((0,), (0,)))
            for t in range(stop, count):
                rows[t] = jnp.where(lane < stop * SUB, 0.0, rows[t]) - drop[t * SUB : (t + 1) * SUB]


def pair_of(v):
    return jnp.concatenate(split(v), axis=1)


def weights(pair):
    hi, lo = pair[:, :LANES], pair[:, LANES:]
    return jnp.concatenate(
        [jnp.concatenate([hi, hi], axis=1), jnp.concatenate([lo, jnp.zeros_like(lo)], axis=1)], axis=0
    )


def folded(pair, weight):
    both = contract(pair, weight, NT)
    half = both.shape[1] // 2
    return both[:, :half] + both[:, half:]


def factor_panels(work_ref, pair_ref, weight_ref, inverse_ref):
    def panel(p, carry):
        mine = pl.ds(pl.multiple_of(p * LANES, LANES), LANES)

        for c in range(1, work_ref.shape[0]):

            @pl.when(p == c)
            def _(c=c):
                first = c * LANES
                value = work_ref[c, first:, :]
                for k in range(c):
                    value = value - folded(
                        pair_ref[k, first:, :], weights(pair_ref[k, first : first + LANES, :])
                    )
                work_ref[c, first:, :] = value

        inverse_factor(work_ref[p, mine, :], inverse_ref)
        weight = weights(pair_of(inverse_ref[...]))
        solved = folded(pair_of(work_ref[p]), weight)
        weight_ref[p] = weight
        pair_ref[p] = pair_of(solved)
        work_ref[p] = solved
        return carry

    lax.fori_loop(0, work_ref.shape[0], panel, 0)


def packed_block(gram_ref, row, col, panels):
    at = sum(panels - p for p in range(col)) + row - col
    return gram_ref[at * LANES : (at + 1) * LANES, :]


def factor_kernel(scale, gram_ref, rows_ref, out_ref, work_ref, pair_ref, weight_ref, inverse_ref):
    panels = work_ref.shape[0]
    size = panels * LANES
    for p in range(panels):
        for r in range(panels):
            block = packed_block(gram_ref, r, p, panels) * scale if r >= p else jnp.zeros((LANES, LANES), F32)
            work_ref[p, r * LANES : (r + 1) * LANES, :] = block
        work_ref[p, size:, :] = rows_ref[:, p * LANES : (p + 1) * LANES]
    factor_panels(work_ref, pair_ref, weight_ref, inverse_ref)
    for p in range(panels):
        out_ref[:, p * LANES : (p + 1) * LANES] = work_ref[p, size:, :]


def factor_all(gram, rows, scale):
    count, width = rows.shape
    panels = width // LANES
    scratch = [
        pltpu.VMEM((panels, width + count, LANES), F32),
        pltpu.VMEM((panels, width + count, 2 * LANES), BF16),
        pltpu.VMEM((panels, 2 * LANES, 2 * LANES), BF16),
        pltpu.VMEM((LANES, LANES), F32),
    ]
    return kernel_call(lambda *refs: factor_kernel(scale, *refs), f32(count, width), scratch)(gram, rows)


def quarter_block(ref, second, at):
    part, at = divmod(at, ref.shape[2] // LANES)
    return ref[part, second, at * LANES : (at + 1) * LANES, :]


def cross_block(ref, second, at):
    rows = ref.shape[3] // LANES
    part, at = divmod(at, ref.shape[1] * rows)
    piece, at = divmod(at, rows)
    return ref[part, piece, second, at * LANES : (at + 1) * LANES, :]


def triangle_block(ref, second, row, col, panels):
    return quarter_block(ref, second, sum(panels - p for p in range(col)) + row - col)


def first_kernel(scale, tri_ref, rows_ref, out_ref, pair_ref, weight_ref, work_ref, inverse_ref):
    panels = work_ref.shape[0]
    size = panels * LANES
    for p in range(panels):
        for r in range(panels):
            block = jnp.zeros((LANES, LANES), F32)
            if r >= p:
                block = triangle_block(tri_ref, 0, r, p, panels) * scale
            work_ref[p, r * LANES : (r + 1) * LANES, :] = block
        work_ref[p, size:, :] = rows_ref[:, p * LANES : (p + 1) * LANES]
    factor_panels(work_ref, pair_ref, weight_ref, inverse_ref)
    for p in range(panels):
        out_ref[:, p * LANES : (p + 1) * LANES] = work_ref[p, size:, :]


def second_kernel(
    scale, tri_ref, cross_ref, rows_ref, done_ref, pair_ref, weight_ref,
    out_ref, work_ref, left_ref, new_pair_ref, new_weight_ref, inverse_ref,
):
    panels = work_ref.shape[0]
    size = panels * LANES
    half = panels // 2
    for p in range(panels):
        blocks = []
        for r in range(panels):
            second, inner = divmod(r, half)
            blocks.append(cross_block(cross_ref, second, p * half + inner))
        solve = jnp.concatenate(blocks, axis=0) * scale
        for k in range(p):
            pair = left_ref[:size, 2 * k * LANES : 2 * (k + 1) * LANES]
            solve = solve - folded(pair, weights(pair_ref[k, p * LANES : (p + 1) * LANES, :]))
        span = slice(2 * p * LANES, 2 * (p + 1) * LANES)
        left_ref[:size, span] = pair_of(folded(pair_of(solve), weight_ref[p]))
        left_ref[size:, span] = pair_ref[p, size:, :]
    for p in range(panels):
        mine = left_ref[p * LANES : (p + 1) * LANES, :]
        weight = jnp.concatenate(
            [weights(mine[:, 2 * k * LANES : 2 * (k + 1) * LANES]) for k in range(panels)], axis=1
        )
        drop = folded(left_ref[p * LANES :, :], weight)
        for r in range(panels):
            block = jnp.zeros((LANES, LANES), F32)
            if r >= p:
                block = triangle_block(tri_ref, 1, r, p, panels) * scale - drop[(r - p) * LANES : (r - p + 1) * LANES]
            work_ref[p, r * LANES : (r + 1) * LANES, :] = block
        work_ref[p, size:, :] = rows_ref[:, size + p * LANES : size + (p + 1) * LANES] - drop[size - p * LANES :]
    factor_panels(work_ref, new_pair_ref, new_weight_ref, inverse_ref)
    out_ref[:, :size] = done_ref[...]
    for p in range(panels):
        out_ref[:, size + p * LANES : size + (p + 1) * LANES] = work_ref[p, size:, :]


def factor_halves(tri, cross, rows, scale):
    count, width = rows.shape
    size = width // 2
    panels = size // LANES
    total = size + count
    pairs, weight = (panels, total, 2 * LANES), (panels, 2 * LANES, 2 * LANES)
    work = [pltpu.VMEM((panels, total, LANES), F32)]
    inverse = [pltpu.VMEM((LANES, LANES), F32)]
    done, pair, mult = kernel_call(
        lambda *refs: first_kernel(scale, *refs),
        [f32(count, size), bf16(*pairs), bf16(*weight)],
        work + inverse,
    )(tri, rows)
    more = [pltpu.VMEM((total, panels * 2 * LANES), BF16), pltpu.VMEM(pairs, BF16), pltpu.VMEM(weight, BF16)]
    return kernel_call(
        lambda *refs: second_kernel(scale, *refs), f32(count, width), work + more + inverse
    )(tri, cross, rows, done, pair, mult)


def any_orb(part, top, scale):
    halo = top.shape[0]
    current = jnp.concatenate([part[:halo] + top, part[halo:]], axis=0)
    rows = lax.all_to_all(current, "orb", split_axis=0, concat_axis=1, tiled=True)
    panels = rows.shape[1] // LANES
    packed = LANES * panels * (panels + 1) // 2
    gram = kernel_call(gram_kernel, f32(packed, LANES))(rows)
    dom = bits("dom")
    return factor_all(summed(gram, dom[:1] + bits("orb") + dom[1:]), rows, scale)


def two_orb(part, top, scale):
    own, cols = part.shape
    halo = top.shape[0]
    second = lax.axis_index("orb")
    panels = cols // LANES
    packed = LANES * (panels * (panels + 1) // 2 + panels * (panels // 2))
    flag = second.reshape(1)
    low = exchanged(part[halo:], "orb", 1)
    gram = low_gram(flag, part, low, halo, packed)
    high = exchanged(part[:halo] + top, "orb", 1)
    dom = bits("dom")
    stages = dom if len(dom) < 4 else dom[:-2] + [("dom", dom[-2][1], 4)]
    flags = jnp.stack([rank(*stages[0]), second])
    keep, send = high_gram(flags, part, top, high, gram)
    gram = scattered(keep + exchanged(send, "dom", stages[0][1]), stages[1:])
    cut = LANES * panels * (panels + 1) // 2 // lax.axis_size("dom")
    orb = ("orb", 1, 2)
    tri = everywhere(gram[:cut], stages[:0:-1] + [orb, stages[0]])
    cross = everywhere(gram[cut:], stages[:1:-1] + [orb, stages[1], stages[0]])
    tri = tri.reshape(2, 2, -1, LANES)
    cross = cross.reshape(2, stages[1][2], 2, -1, LANES)
    mine = jnp.concatenate([part[:halo] + top, part[halo:]], axis=0).reshape(2, own // 2, cols)
    other = jnp.concatenate([high, low], axis=0).reshape(2, own // 2, cols)
    mine = jnp.where(second == 0, mine[0], mine[1])
    other = jnp.where(second == 0, other[0], other[1])
    rows = jnp.where(
        second == 0, jnp.concatenate([mine, other], axis=1), jnp.concatenate([other, mine], axis=1)
    )
    return factor_halves(tri, cross, rows, scale)


def everywhere(block, stages):
    for stage in stages:
        block = gathered(block, stage).reshape(-1, LANES)
    return block


def with_flag(body, out_shape, count, scratch=()):
    specs = [pl.BlockSpec(memory_space=pltpu.SMEM)] + [pl.BlockSpec(memory_space=pltpu.VMEM)] * count
    return pl.pallas_call(
        body,
        out_shape=out_shape,
        in_specs=specs,
        scratch_shapes=list(scratch),
        compiler_params=pltpu.CompilerParams(vmem_limit_bytes=VMEM_BYTES),
    )


def low_gram(flag, part, low, halo, packed):
    kernel = lambda *refs: low_gram_kernel(halo, *refs)
    return with_flag(kernel, f32(packed, LANES), 2)(flag, part, low)


def high_gram(flags, part, top, high, gram):
    kernel = lambda *refs: high_gram_kernel(lax.axis_size("dom"), *refs)
    outs = [f32(gram.shape[0] // 2, LANES)] * 2
    return with_flag(kernel, outs, 4, [pltpu.VMEM(gram.shape, F32)])(flags, part, top, high, gram)


def body(orbitals, cell_mats, cell_map):
    own, cols = orbitals.shape
    size = cell_mats.shape[1]
    node_total = own * lax.axis_size("dom")
    matrix = kernel_call(order_kernel, [bf16(size, size)] * 2)(cell_map, cell_mats)
    part, top = filtered_columns(orbitals, matrix)
    panels = cols // LANES
    two = (
        lax.axis_size("orb") == 2
        and lax.axis_size("dom") > 2
        and cols % (2 * LANES) == 0
        and (LANES * panels * (panels + 1) // 2) % lax.axis_size("dom") == 0
        and panels * panels // 2 % 4 == 0
        and (LANES * panels * panels // 2) % lax.axis_size("dom") == 0
    )
    return (two_orb if two else any_orb)(part, top, 1.0 / node_total)


def solution(mesh):
    placed = (P("dom", "orb"), P("dom", None, None), P("dom", None))
    return jax.shard_map(
        body, mesh=mesh, in_specs=placed, out_specs=P(("dom", "orb"), None), check_vma=False
    )
```
